32 devices in a mesh: ctx: 4 (over y, core), head: 2 (over x), batch: 4 (over z).
Axes of the slice: x: 2, y: 2, z: 4, core: 2. Of those that a mesh axis runs over, the one named last changes fastest.
Arguments:
- ingest: bfloat16 [4, 4, 12, 128, 4, 256], P('ctx', 'batch', None, None, None, 'head'), may hold values from -6 to 6
- src_shard: int32 [4, 4, 6], P('ctx'), may hold values from 0 to 3, as said below
- src_slot: int32 [4, 4, 6], P('ctx'), may hold values from 0 to 11
- hist_len: int32 [4, 4], P('batch'), may hold values from 1 to 1536, 3072 in all within a row
- w_out: bfloat16 [256, 256], P('head'), may hold values from -0.375 to 0.375
Outputs:
- mixed: bfloat16 [4, 3072, 256], P('batch', 'ctx', 'head')
The draws below stay inside these ranges and needn't reach their ends.
Inputs may be any that keep to these rules, and one draw needn't show every extreme that they name: `src_shard`: for each owner index, every owner's 6 blocks come from exactly two different ingestion shards, 3 from each; no (shard, slot) pair of one owner index feeds two blocks. `hist_len`: the 4 histories of a group fill its 3072 positions in order.
All inputs are finite; a program needn't handle non-finite values.
Results may differ from the reference program's by a relative error of at most 0.0058.
Values may be sent and summed in bfloat16 or wider, within the bound.
A program may use at most 64 MiB of HBM per device.

```python
import math
import jax
import jax.numpy as jnp
import numpy as np
from jax import lax

HD = 128
HEADS = 2
D = 256
BLOCK = 128
BLK_DEV = 6
CAP = 3
GROUPS = 4
CTXS = 4
SLOTS = 12
ROWS_DEV = 768
SEQ = 3072
USERS = 4
HIST_MOST = 1536


def plan_blocks(key):

    def one_ctx(ctx_key):
        key_sources, key_slots, key_order = jax.random.split(ctx_key, 3)
        source_order = jax.vmap(lambda one_key: jax.random.permutation(one_key, GROUPS))(jax.random.split(key_sources, GROUPS))
        sources = source_order[:, :2].astype(jnp.int32)
        requests = sources.reshape(-1)
        request_pos = jnp.arange(2 * GROUPS)
        earlier = (requests[None, :] == requests[:, None]) & (request_pos[None, :] < request_pos[:, None])
        request_rank = jnp.sum(earlier.astype(jnp.int32), axis=1)
        slot_orders = jax.vmap(lambda one_key: jax.random.permutation(one_key, SLOTS))(jax.random.split(key_slots, GROUPS))
        wanted = request_rank[:, None] * CAP + jnp.arange(CAP, dtype=jnp.int32)[None, :]
        chosen_slots = jnp.take_along_axis(slot_orders[requests], wanted, axis=1)
        owner_slots = chosen_slots.reshape(GROUPS, BLK_DEV).astype(jnp.int32)
        owner_shards = jnp.repeat(sources, CAP, axis=1)
        block_order = jax.vmap(lambda one_key: jax.random.permutation(one_key, BLK_DEV))(jax.random.split(key_order, GROUPS))
        return (jnp.take_along_axis(owner_shards, block_order, axis=1), jnp.take_along_axis(owner_slots, block_order, axis=1))
    return jax.vmap(one_ctx)(jax.random.split(jax.random.fold_in(key, 7), CTXS))


def draw_src_shard(key, part):
    return plan_blocks(key)[0].astype(jnp.int32)


def draw_src_slot(key, part):
    return plan_blocks(key)[1].astype(jnp.int32)


def block_scale(own_key, shape, cuts, least, largest):
    def one(axis_at, blocks):
        heights = jax.random.uniform(jax.random.fold_in(jax.random.fold_in(own_key, 6), axis_at), (blocks,), jnp.float32, least / len(cuts), largest / len(cuts))
        return jnp.repeat(jnp.exp(heights), shape[axis_at] // blocks).reshape((-1,) + (1,) * (len(shape) - axis_at - 1))

    gain = one(*cuts[0])
    for cut in cuts[1:]:
        gain = gain * one(*cut)
    return gain


def profile(count, total, most, lean):
    loads = [(1 << 20) // math.isqrt(rank ** lean) + 1 for rank in range(2, count + 1)]
    spare, holding = total - most - (count - 1), [1] * (count - 1)
    while spare > 0:
        free = [i for i in range(count - 1) if holding[i] < most]
        mass, remaining = sum([loads[i] for i in free]), spare
        for i in free:
            addition = min(most - holding[i], max(1, remaining * loads[i] // mass), spare)
            holding[i] = holding[i] + addition
            spare = spare - addition
    return np.array([most] + holding)


def ragged(key, amount, total, most, slope):
    if amount == 2:
        one = jax.random.randint(key, (), max(1, total - most), min(most, total - 1) + 1)
        return jnp.stack([one, total - one])
    sizes = jnp.asarray(profile(amount, total, most, slope), jnp.int32)
    twos = (amount - 1) // 2
    source_of, receiver = sizes[1:1 + 2 * twos:2], sizes[2:2 + 2 * twos:2]
    room = jnp.minimum(source_of - 1, most - receiver)
    shifted = jax.random.randint(jax.random.fold_in(key, 1), (twos,), 0, 1 << 20) % (room + 1)
    sizes = sizes.at[1:1 + 2 * twos:2].set(source_of - shifted).at[2:2 + 2 * twos:2].set(receiver + shifted)
    return sizes[jax.random.permutation(jax.random.fold_in(key, 2), amount)]


def centred(own_key, shape, spread, reach, cuts=(), held_as=jnp.bfloat16):
    loudness = block_scale(own_key, shape, cuts, -0.22, 0.18) if cuts else 1.0
    array = jax.random.normal(own_key, shape, jnp.float32) * spread * loudness
    return jnp.minimum(jnp.maximum(array, -reach), reach).astype(held_as)


def setup_inputs(seed: int = 0) -> dict:
    keys = jax.random.split(jax.random.key(seed), 6)
    return {
        "ingest": centred(keys[0], (CTXS, GROUPS, SLOTS, BLOCK, 4, D), 1.0, 6.0, ((0, 4), (1, 4), (5, 2))),
        "src_shard": draw_src_shard(jax.random.fold_in(keys[5], 71), 0),
        "src_slot": draw_src_slot(jax.random.fold_in(keys[5], 71), 0),
        "hist_len": jax.vmap(lambda own: ragged(own, USERS, SEQ, HIST_MOST, 2))(jax.random.split(keys[3], GROUPS)).reshape((GROUPS, USERS)).astype(jnp.int32),
        "w_out": centred(keys[4], (D, D), D ** -0.5, 0.375, ((0, 2),)),
    }


def reference(ingest, src_shard, src_slot, hist_len, w_out):
    ctx_ids = jnp.arange(CTXS, dtype=jnp.int32)[:, None, None]
    owned = ingest[ctx_ids, src_shard, src_slot]
    owned = jnp.transpose(owned, (1, 0, 2, 3, 4, 5)).reshape(GROUPS, SEQ, 4, HEADS, HD)
    score_scale = 1.0 / math.sqrt(HD)

    def per_group(group_args):
        group_rows, lengths = group_args
        seg_ends = jnp.cumsum(lengths).astype(jnp.int32)
        all_pos = jnp.arange(SEQ, dtype=jnp.int32)
        segment = lax.optimization_barrier(jnp.sum((all_pos[:, None] >= seg_ends[None, :]).astype(jnp.int32), axis=1))
        key_rows = group_rows[:, 1].astype(jnp.float32)
        value_rows = group_rows[:, 2].astype(jnp.float32)

        def per_block(offset):
            query_rows = lax.dynamic_slice_in_dim(group_rows, offset, ROWS_DEV, 0)
            query_pos = offset + jnp.arange(ROWS_DEV, dtype=jnp.int32)
            query_seg = lax.dynamic_slice_in_dim(segment, offset, ROWS_DEV, 0)
            scores = jnp.einsum('qhd,khd->hqk', query_rows[:, 0].astype(jnp.float32), key_rows) * score_scale
            visible = (query_seg[:, None] == segment[None, :]) & (all_pos[None, :] <= query_pos[:, None])
            weights = jnp.where(visible[None], jax.nn.silu(scores), 0.0).astype(jnp.bfloat16)
            weights = lax.optimization_barrier(weights).astype(jnp.float32)
            attended = jnp.einsum('hqk,khd->qhd', weights, value_rows)
            mean_square = lax.optimization_barrier(jnp.mean(attended * attended, axis=-1, keepdims=True))
            normed = attended * lax.rsqrt(mean_square + 1e-06)
            gated = (normed * query_rows[:, 3].astype(jnp.float32)).astype(jnp.bfloat16).reshape(ROWS_DEV, D)
            return jnp.dot(gated, w_out, preferred_element_type=jnp.float32).astype(jnp.bfloat16)
        offsets = jnp.arange(CTXS, dtype=jnp.int32) * ROWS_DEV
        return lax.map(per_block, offsets).reshape(SEQ, D)
    return lax.map(per_group, (owned, hist_len))
```

```python
import functools
import math

import jax
import jax.numpy as jnp
from jax import lax
from jax.experimental import pallas as pl
from jax.experimental.pallas import tpu as pltpu
from jax.sharding import PartitionSpec as P

HD = 128
MESH = pl.DeviceIdType.MESH
QUERY, KEY, VALUE, UPDATE = 0, 1, 2, 3
FIRST_KINDS = (KEY, VALUE, QUERY)


def unit_list(capacity, rows):
    units = [(kind, k) for kind in FIRST_KINDS for k in range(capacity)]
    return units + [(UPDATE, c) for c in range(len(update_chunks(capacity, rows)))]


def update_chunks(capacity, rows):
    half = rows // 2
    return [(k, 0, rows) for k in range(capacity - 1)] + [(capacity - 1, 0, half), (capacity - 1, half, half)]


def kernel(sizes, shard_hbm, slot_hbm, hist_hbm, ingest_hbm, w_hbm, out_ref,
           shard_ref, slot_ref, hist_ref, w_ref, local_sems,
           ingest_ref,
           send_bufs, send_u, recv_bufs, recv_u, relay_bufs, relay_u, own_k, own_v, own_q, prev_k, prev_v,
           start_ref, att, gated, w_cols, mixed,
           z_send, z_recv, c_send, c_recv, h_send, h_recv, w_send, w_recv,
           ingest_sem, from_low, from_high):
    groups, ctxs, heads, per_owner, rows = sizes
    capacity = per_owner // 2
    chunks = update_chunks(capacity, rows)
    window = ctxs // 2
    row_count = per_owner * rows
    my_group = lax.axis_index("batch")
    my_ctx = lax.axis_index("ctx")
    my_head = lax.axis_index("head")

    barrier = pltpu.get_barrier_semaphore()
    ingest_copy = pltpu.make_async_copy(ingest_hbm, ingest_ref, ingest_sem)
    ingest_copy.start()
    local_copies = [pltpu.make_async_copy(src, dst, local_sems.at[i]) for i, (src, dst) in enumerate((
        (shard_hbm, shard_ref), (slot_hbm, slot_ref), (hist_hbm, hist_ref), (w_hbm, w_ref)))]
    for copy in local_copies:
        copy.start()
    for axis, me, count in (("ctx", my_ctx, ctxs), ("head", my_head, heads)):
        for offset in range(1, count):
            pl.semaphore_signal(barrier, inc=1, device_id={axis: lax.rem(me + offset, count)}, device_id_type=MESH)
    has_low, has_high = my_group > 0, my_group < groups - 1

    def tell(there, semaphore, to):
        @pl.when(there)
        def _():
            pl.semaphore_signal(semaphore, inc=1, device_id={"batch": to}, device_id_type=MESH)

    tell(has_low, barrier, my_group - 1)
    tell(has_high, barrier, my_group + 1)
    neighbours = jnp.where(has_low, 1, 0) + jnp.where(has_high, 1, 0)

    for copy in local_copies:
        copy.wait()
    slots = []
    for dst in range(groups):
        picked = [jnp.int32(0)] * capacity
        seen = jnp.int32(0)
        for j in range(per_owner):
            hit = shard_ref[dst, j] == my_group
            slot = slot_ref[dst, j]
            for k in range(capacity):
                picked[k] = jnp.where(hit & (seen == k), slot, picked[k])
            seen = seen + jnp.where(hit, 1, 0)
        slots.append(picked)

    sources = [shard_ref[my_group, j] for j in range(per_owner)]
    ranks, sides = [], []
    for j in range(per_owner):
        rank = jnp.int32(0)
        for i in range(j):
            rank = rank + jnp.where(sources[i] == sources[j], 1, 0)
        ranks.append(jnp.minimum(rank, capacity - 1))
        sides.append(jnp.where(sources[j] == sources[0], 0, 1))

    def split_kind(kind):
        width = 4 * rows
        row = lax.broadcasted_iota(jnp.int32, (rows, width), 0)
        col = lax.broadcasted_iota(jnp.int32, (rows, width), 1)
        pick = jnp.where(col == row * 4 + kind, 1.0, 0.0).astype(jnp.bfloat16)

        def one(dst, k):
            block = ingest_ref[slots[dst][k]]
            return jnp.dot(pick, block, preferred_element_type=jnp.float32).astype(jnp.bfloat16)

        return one

    units = unit_list(capacity, rows)
    half = groups // 2
    low_side = my_group < half
    depth = jnp.where(low_side, half - 1 - my_group, my_group - half)

    def same(e):
        return jnp.where(low_side, half - 1 - e, half + e)

    def other(e):
        return jnp.where(low_side, half + e, half - 1 - e)

    def fill(kind, k):
        one = split_kind(kind)
        for dst in range(groups):
            block = one(dst, k)
            if kind == UPDATE:
                for c, (of, low, size) in enumerate(chunks):
                    if of == k:
                        send_u[c][dst] = block[low:low + size]
            else:
                send_bufs[FIRST_KINDS.index(kind), dst, k] = block

    def keep(kind):
        if kind == UPDATE:
            for c in range(len(chunks)):
                recv_u[c][my_group] = send_u[c][my_group]
        else:
            n = FIRST_KINDS.index(kind)
            recv_bufs[n][my_group] = send_bufs[n, my_group]

    def outbox(n, dst):
        kind, c = units[n]
        return send_u[c].at[dst] if kind == UPDATE else send_bufs.at[FIRST_KINDS.index(kind), dst, c]

    def inbox(n, src):
        kind, c = units[n]
        return recv_u[c].at[src] if kind == UPDATE else recv_bufs[FIRST_KINDS.index(kind)].at[src, c]

    def relay(n, far, e):
        kind, c = units[n]
        return relay_u[c].at[far - 1, e] if kind == UPDATE else relay_bufs[FIRST_KINDS.index(kind)].at[far - 1, e, c]

    def z_copy(src, dst, n, out_id, in_id, to):
        return pltpu.make_async_remote_copy(
            src_ref=src, dst_ref=dst, send_sem=z_send.at[n, out_id], recv_sem=z_recv.at[n, in_id],
            device_id={"batch": to}, device_id_type=MESH)

    def side_copy(n, here, e):
        return z_copy(outbox(n, same(e)), inbox(n, my_group), n, e, here, same(e))

    def cross_copy(n, e):
        return z_copy(outbox(n, other(e)), inbox(n, my_group), n, half + e, half, other(e))

    def relay_copy(n, here, e):
        return z_copy(outbox(n, other(e)), relay(n, here, e), n, half + e, 2 * half + (here - 1) * half + e, same(0))

    def forward_copy(n, far, e):
        return z_copy(relay(n, far, e), inbox(n, same(far)), n, 2 * half + (far - 1) * half + e, half + far, other(e))

    def side(n, middle):
        for here in range(half):
            if (here == 0) == middle and half > 1:
                @pl.when(depth == here)
                def _():
                    for e in range(half):
                        if e != here:
                            side_copy(n, here, e).start()

    def cross(n, e):
        @pl.when(depth == 0)
        def _():
            cross_copy(n, e).start()

    def to_middle(n, e):
        for here in range(1, half):
            @pl.when(depth == here)
            def _():
                relay_copy(n, here, e).start()

    def forward(n, e):
        for far in range(1, half):
            @pl.when(depth == 0)
            def _():
                relay_copy(n, far, e).wait_recv()
                forward_copy(n, far, e).start()

    def arrive(n):
        for e in range(half):
            @pl.when(depth != e)
            def _():
                side_copy(n, e, e).wait_recv()
            z_copy(inbox(n, other(e)), inbox(n, other(e)), n, half + e, half + e, other(e)).wait_recv()

    def sent(n):
        for e in range(half):
            @pl.when(depth != e)
            def _():
                side_copy(n, e, e).wait_send()
            cross_copy(n, e).wait_send()
        for far in range(1, half):
            @pl.when(depth == 0)
            def _():
                for e in range(half):
                    forward_copy(n, far, e).wait_send()

    def collect(kind, own_ref):
        n = FIRST_KINDS.index(kind)
        for k in range(capacity):
            arrive(n * capacity + k)
        for j in range(per_owner):
            own_ref[j * rows:(j + 1) * rows, :] = recv_bufs[n][sources[j], ranks[j]]

    def hear(distance):
        for there, semaphore in ((my_group >= distance, from_low), (my_group + distance < groups, from_high)):
            @pl.when(there)
            def _():
                pl.semaphore_wait(semaphore.at[distance], 1)

    def pass_on(distance):
        tell((my_group >= distance) & has_high, from_low.at[distance + 1], my_group + 1)
        tell((my_group + distance < groups) & has_low, from_high.at[distance + 1], my_group - 1)

    key_units, value_units, query_units = ([n for n, (kind, _) in enumerate(units) if kind == want] for want in FIRST_KINDS)
    update_units = list(range(3 * capacity, len(units)))
    pairs = key_units + value_units
    far_first = list(range(half - 1, -1, -1))

    ingest_copy.wait()
    fill(KEY, 0)
    pl.semaphore_wait(barrier, neighbours + ctxs + heads - 2)
    for n in pairs:
        if n > 0:
            fill(*units[n])
        if n == 1:
            for distance in range(1, half):
                if distance > 1:
                    hear(distance)
                pass_on(distance)
        cross(n, 0)
        to_middle(n, 0)
        side(n, True)
    for e in range(1, half):
        for n in pairs:
            to_middle(n, e)
    for n in pairs:
        side(n, False)
    for n in query_units:
        fill(QUERY, units[n][1])
        side(n, True)
    for k in range(capacity):
        fill(UPDATE, k)
    for n in update_units:
        side(n, True)
    for group in (query_units, update_units):
        for e in far_first:
            for n in group:
                to_middle(n, e)
        for n in group:
            side(n, False)
    for kind in (*FIRST_KINDS, UPDATE):
        keep(kind)
    if half > 1:
        hear(half)
    for n in pairs:
        forward(n, 0)
    for e in range(1, half):
        for group in (key_units, value_units):
            for n in group:
                cross(n, e)
            for n in group:
                forward(n, e)

    w_copies = []
    for offset in range(1, heads):
        to = lax.rem(my_head + offset, heads)
        copy = pltpu.make_async_remote_copy(
            src_ref=w_ref.at[:, pl.ds(pl.multiple_of(to * HD, HD), HD)], dst_ref=w_cols.at[my_head],
            send_sem=w_send.at[offset], recv_sem=w_recv.at[offset],
            device_id={"head": to}, device_id_type=MESH)
        copy.start()
        w_copies.append(copy)
    w_cols[my_head] = w_ref[:, pl.ds(pl.multiple_of(my_head * HD, HD), HD)]

    ends, total = [], jnp.int32(0)
    for u in range(hist_ref.shape[0]):
        total = total + hist_ref[u]
        ends.append(total)
    base = my_ctx * row_count
    position = base + lax.broadcasted_iota(jnp.int32, (row_count, HD), 0)
    first = jnp.zeros((row_count, HD), jnp.int32)
    for end in ends:
        first = jnp.where(position >= end, end, first)
    start_ref[...] = first - base

    def ctx_copy(n, own_ref, prev_ref, offset):
        return pltpu.make_async_remote_copy(
            src_ref=own_ref, dst_ref=prev_ref.at[offset - 1],
            send_sem=c_send.at[n, offset - 1], recv_sem=c_recv.at[n, offset - 1],
            device_id={"ctx": lax.rem(my_ctx + offset, ctxs)}, device_id_type=MESH)

    def push(n, own_ref, prev_ref):
        for offset in range(1, window + 1):
            @pl.when(my_ctx + offset < ctxs)
            def _():
                ctx_copy(n, own_ref, prev_ref, offset).start()

    collect(KEY, own_k)
    push(0, own_k, prev_k)
    collect(VALUE, own_v)
    push(1, own_v, prev_v)
    for group in (query_units, update_units):
        for e in far_first:
            for n in group:
                cross(n, e)
                forward(n, e)
    collect(QUERY, own_q)

    tile = 2 * rows if per_owner % 2 == 0 else rows
    tiles = row_count // tile
    half_scale = 0.5 / math.sqrt(HD)

    def attend(q, key_tile, value_tile, q_lo, k_lo, shift, causal):
        scores = lax.dot_general(q, key_tile, (((1,), (1,)), ((), ())), preferred_element_type=jnp.float32)
        half = scores * half_scale
        act = half + half * jnp.tanh(half)
        key_pos = lax.broadcasted_iota(jnp.int32, (tile, tile), 1) + (k_lo - shift)
        first_pos = jnp.concatenate([start_ref[q_lo:q_lo + tile, :]] * (tile // HD), axis=1)
        visible = key_pos >= first_pos
        if causal:
            visible = visible & (key_pos <= lax.broadcasted_iota(jnp.int32, (tile, tile), 0) + q_lo)
        weights = jnp.where(visible, act, 0.0).astype(jnp.bfloat16)
        return jnp.dot(weights, value_tile, preferred_element_type=jnp.float32)

    def put(i, value, add):
        for part in range(tile // rows):
            at = i * (tile // rows) + part
            piece = value[part * rows:(part + 1) * rows]
            att[at] = att[at] + piece if add else piece

    for i in range(tiles):
        q = own_q[i * tile:(i + 1) * tile, :]
        acc = None
        for t in range(i + 1):
            span = slice(t * tile, (t + 1) * tile)
            term = attend(q, own_k[span, :], own_v[span, :], i * tile, t * tile, 0, t == i)
            acc = term if acc is None else acc + term
        put(i, acc, False)
    for offset in range(1, window + 1):
        @pl.when(my_ctx >= offset)
        def _():
            ctx_copy(0, own_k, prev_k, offset).wait_recv()
            ctx_copy(1, own_v, prev_v, offset).wait_recv()
            for i in range(tiles):
                q = own_q[i * tile:(i + 1) * tile, :]
                acc = None
                for t in range(i if offset == window else 0, tiles):
                    span = slice(t * tile, (t + 1) * tile)
                    term = attend(q, prev_k[offset - 1, span, :], prev_v[offset - 1, span, :],
                                  i * tile, t * tile, offset * row_count, False)
                    acc = term if acc is None else acc + term
                put(i, acc, True)

    source_other = sources[0]
    for j in range(1, per_owner):
        source_other = jnp.where(sides[j] == 1, sources[j], source_other)
    side_source = (sources[0], source_other)
    h_copies = []
    for c, (k, low, size) in enumerate(chunks):
        arrive(update_units[c])
        for part in range(2):
            at = jnp.int32(0)
            for j in range(per_owner):
                at = jnp.where((ranks[j] == k) & (sides[j] == part), j, at)
            rows_f32 = att[at, low:low + size, :]
            mean_square = jnp.mean(rows_f32 * rows_f32, axis=-1, keepdims=True)
            normed = rows_f32 * lax.rsqrt(mean_square + 1e-06)
            update = recv_u[c][side_source[part]].astype(jnp.float32)
            gated[c][my_head, part * size:(part + 1) * size, :] = (normed * update).astype(jnp.bfloat16)
        for offset in range(1, heads):
            copy = pltpu.make_async_remote_copy(
                src_ref=gated[c].at[my_head], dst_ref=gated[c].at[my_head],
                send_sem=h_send.at[c, offset], recv_sem=h_recv.at[c, offset],
                device_id={"head": lax.rem(my_head + offset, heads)}, device_id_type=MESH)
            copy.start()
            h_copies.append(copy)
    for copy in w_copies:
        copy.wait()
    for n in range(len(units)):
        sent(n)
    for c, (k, low, size) in enumerate(chunks):
        for copy in h_copies[c * (heads - 1):(c + 1) * (heads - 1)]:
            copy.wait()
        acc = None
        for h in range(heads):
            term = jnp.dot(gated[c][h], w_cols[h], preferred_element_type=jnp.float32)
            acc = term if acc is None else acc + term
        acc = acc.astype(jnp.bfloat16)
        for side in range(2):
            mixed[2 * k + side, low:low + size, :] = acc[side * size:(side + 1) * size]
    for j in range(per_owner):
        out_ref[j * rows:(j + 1) * rows, :] = mixed[2 * ranks[j] + sides[j]]
    for offset in range(1, window + 1):
        @pl.when(my_ctx + offset < ctxs)
        def _():
            ctx_copy(0, own_k, prev_k, offset).wait_send()
            ctx_copy(1, own_v, prev_v, offset).wait_send()


def body(ingest, src_shard, src_slot, hist_len, w_out):
    groups, ctxs, heads = (lax.axis_size(a) for a in ("batch", "ctx", "head"))
    slot_total, rows, kinds, width = ingest.shape[2:]
    per_owner = src_shard.shape[2]
    capacity = per_owner // 2
    chunks = update_chunks(capacity, rows)
    units, half = len(unit_list(capacity, rows)), groups // 2
    spans = max(half - 1, 1)
    window = ctxs // 2
    row_count = per_owner * rows
    bf16 = jnp.bfloat16
    dma = pltpu.SemaphoreType.DMA
    vmem = pl.BlockSpec(memory_space=pltpu.VMEM)
    mixed = pl.pallas_call(
        functools.partial(kernel, (groups, ctxs, heads, per_owner, rows)),
        out_shape=pltpu.VMEM((row_count, width), bf16),
        in_specs=[pl.BlockSpec(memory_space=pl.ANY)] * 5,
        out_specs=vmem,
        scratch_shapes=[
            pltpu.SMEM(src_shard.shape[1:], jnp.int32), pltpu.SMEM(src_slot.shape[1:], jnp.int32),
            pltpu.SMEM(hist_len.shape[1:], jnp.int32), pltpu.VMEM(w_out.shape, bf16), dma((4,)),
            pltpu.VMEM((slot_total, rows * kinds, width), bf16),
            pltpu.VMEM((3, groups, capacity, rows, width), bf16),
            [pltpu.VMEM((groups, size, width), bf16) for _, _, size in chunks],
            [pltpu.VMEM((groups, capacity, rows, width), bf16)] * 3,
            [pltpu.VMEM((groups, size, width), bf16) for _, _, size in chunks],
            [pltpu.VMEM((spans, half, capacity, rows, width), bf16)] * 3,
            [pltpu.VMEM((spans, half, size, width), bf16) for _, _, size in chunks],
            pltpu.VMEM((row_count, width), bf16),
            pltpu.VMEM((row_count, width), bf16),
            pltpu.VMEM((row_count, width), bf16),
            pltpu.VMEM((window, row_count, width), bf16),
            pltpu.VMEM((window, row_count, width), bf16),
            pltpu.VMEM((row_count, width), jnp.int32),
            pltpu.VMEM((per_owner, rows, width), jnp.float32),
            [pltpu.VMEM((heads, 2 * size, width), bf16) for _, _, size in chunks],
            pltpu.VMEM((heads, width, width), bf16),
            pltpu.VMEM((per_owner, rows, width), bf16),
            dma((units, groups + spans * half)), dma((units, groups + spans * half)),
            dma((2, window)), dma((2, window)),
            dma((len(chunks), heads)), dma((len(chunks), heads)),
            dma((heads,)), dma((heads,)),
            dma, pltpu.SemaphoreType.REGULAR((groups,)), pltpu.SemaphoreType.REGULAR((groups,)),
        ],
        compiler_params=pltpu.CompilerParams(
            collective_id=0, has_side_effects=True, vmem_limit_bytes=56 * 1024 * 1024),
    )(src_shard[0], src_slot[0], hist_len[0],
      ingest.reshape(slot_total, rows * kinds, width), w_out)
    return mixed[None]


def solution(mesh):
    in_specs = (
        P("ctx", "batch", None, None, None, "head"),
        P("ctx", None, None),
        P("ctx", None, None),
        P("batch", None),
        P("head", None),
    )
    out_specs = P("batch", "ctx", "head")
    return jax.shard_map(body, mesh=mesh, in_specs=in_specs, out_specs=out_specs, check_vma=False)
```

```python
import functools
import math

import jax
import jax.numpy as jnp
from jax import lax
from jax.experimental import pallas as pl
from jax.experimental.pallas import tpu as pltpu
from jax.sharding import PartitionSpec as P

HD = 128
MESH = pl.DeviceIdType.MESH
QUERY, KEY, VALUE, UPDATE = 0, 1, 2, 3
FIRST_KINDS = (KEY, VALUE, QUERY)
KINDS = (*FIRST_KINDS, UPDATE)
SPREAD = ((9,3),(8,0))


def unit_list(capacity, rows):
    units = [(kind, k) for kind in FIRST_KINDS for k in range(capacity)]
    return units + [(UPDATE, c) for c in range(len(update_chunks(capacity, rows)))]


def update_chunks(capacity, rows):
    chunks, low = [(k, 0, rows) for k in range(capacity - 1)], 0
    for share in (2,4,4):
        chunks.append((capacity - 1, low, rows // share))
        low += rows // share
    return chunks


def kernel(sizes, shard_hbm, slot_hbm, hist_hbm, ingest_hbm, w_hbm, out_ref,
           shard_ref, slot_ref, hist_ref, w_ref, local_sems,
           ingest_ref,
           send_buf, recv_bufs, recv_u, relay_buf, own_k, own_v, own_q, prev_k, prev_v,
           start_ref, att, gated, w_cols, mixed,
           z_send, z_recv, c_send, c_recv, h_send, h_recv, w_send, w_recv,
           ingest_sem, from_low, from_high):
    groups, ctxs, heads, per_owner, rows = sizes
    capacity = per_owner // 2
    chunks = update_chunks(capacity, rows)
    window = ctxs // 2
    row_count = per_owner * rows
    my_group = lax.axis_index("batch")
    my_ctx = lax.axis_index("ctx")
    my_head = lax.axis_index("head")

    barrier = pltpu.get_barrier_semaphore()
    ingest_copy = pltpu.make_async_copy(ingest_hbm, ingest_ref, ingest_sem)
    ingest_copy.start()
    local_copies = [pltpu.make_async_copy(src, dst, local_sems.at[i]) for i, (src, dst) in enumerate((
        (shard_hbm, shard_ref), (slot_hbm, slot_ref), (hist_hbm, hist_ref), (w_hbm, w_ref)))]
    for copy in local_copies:
        copy.start()
    for axis, me, count in (("ctx", my_ctx, ctxs), ("head", my_head, heads)):
        for offset in range(1, count):
            pl.semaphore_signal(barrier, inc=1, device_id={axis: lax.rem(me + offset, count)}, device_id_type=MESH)
    has_low, has_high = my_group > 0, my_group < groups - 1

    def tell(there, semaphore, to):
        @pl.when(there)
        def _():
            pl.semaphore_signal(semaphore, inc=1, device_id={"batch": to}, device_id_type=MESH)

    tell(has_low, barrier, my_group - 1)
    tell(has_high, barrier, my_group + 1)
    neighbours = jnp.where(has_low, 1, 0) + jnp.where(has_high, 1, 0)

    for copy in local_copies:
        copy.wait()
    slots = []
    for dst in range(groups):
        picked = [jnp.int32(0)] * capacity
        seen = jnp.int32(0)
        for j in range(per_owner):
            hit = shard_ref[dst, j] == my_group
            slot = slot_ref[dst, j]
            for k in range(capacity):
                picked[k] = jnp.where(hit & (seen == k), slot, picked[k])
            seen = seen + jnp.where(hit, 1, 0)
        slots.append(picked)

    sources = [shard_ref[my_group, j] for j in range(per_owner)]
    ranks, sides = [], []
    for j in range(per_owner):
        rank = jnp.int32(0)
        for i in range(j):
            rank = rank + jnp.where(sources[i] == sources[j], 1, 0)
        ranks.append(jnp.minimum(rank, capacity - 1))
        sides.append(jnp.where(sources[j] == sources[0], 0, 1))

    def split_kind(kind):
        width = 4 * rows
        row = lax.broadcasted_iota(jnp.int32, (rows, width), 0)
        col = lax.broadcasted_iota(jnp.int32, (rows, width), 1)
        pick = jnp.where(col == row * 4 + kind, 1.0, 0.0).astype(jnp.bfloat16)

        def one(dst, k):
            block = ingest_ref[slots[dst][k]]
            return jnp.dot(pick, block, preferred_element_type=jnp.float32).astype(jnp.bfloat16)

        return one

    units = unit_list(capacity, rows)
    half = groups // 2
    low_side = my_group < half
    depth = jnp.where(low_side, half - 1 - my_group, my_group - half)

    def same(e):
        return jnp.where(low_side, half - 1 - e, half + e)

    def other(e):
        return jnp.where(low_side, half + e, half - 1 - e)

    def fill(kind, k):
        one = split_kind(kind)
        low = (KINDS.index(kind) * capacity + k) * rows
        for dst in range(groups):
            send_buf[dst, low:low + rows, :] = one(dst, k)

    def span(n):
        kind, c = units[n]
        k, low, size = chunks[c] if kind == UPDATE else (c, 0, rows)
        return pl.ds((KINDS.index(kind) * capacity + k) * rows + low, size)

    def inbox(n, src):
        kind, c = units[n]
        return recv_u[c].at[src] if kind == UPDATE else recv_bufs[FIRST_KINDS.index(kind)].at[src, c]

    def keep(kind):
        for n, (of, _) in enumerate(units):
            if of == kind:
                inbox(n, my_group)[...] = send_buf[my_group, span(n), :]

    def z_copy(src, dst, out_id, in_id, to):
        return pltpu.make_async_remote_copy(
            src_ref=src, dst_ref=dst, send_sem=z_send.at[out_id], recv_sem=z_recv.at[in_id],
            device_id={"batch": to}, device_id_type=MESH)

    def here_id(n):
        kind, c = units[n]
        return 3 + c if kind == UPDATE else FIRST_KINDS.index(kind)

    def relay_id(kind, far, e):
        return 3 + len(chunks) + (KINDS.index(kind) * (half - 1) + far - 1) * half + e

    def side_copy(n, e):
        return z_copy(send_buf.at[same(e), span(n)], inbox(n, my_group), e, here_id(n), same(e))

    def cross_copy(n, e):
        return z_copy(send_buf.at[other(e), span(n)], inbox(n, my_group), half + e, here_id(n), other(e))

    def relay_copy(n, far, e):
        return z_copy(send_buf.at[other(e), span(n)], relay_buf.at[far - 1, e, span(n)],
                      half + e, relay_id(units[n][0], far, e), same(0))

    def forward_copy(n, far, e):
        return z_copy(relay_buf.at[far - 1, e, span(n)], inbox(n, same(far)),
                      2 * half + (far - 1) * half + e, here_id(n), other(e))

    def side(n, middle):
        for here in range(half):
            if (here == 0) == middle and half > 1:
                @pl.when(depth == here)
                def _():
                    for e in range(half):
                        if e != here:
                            side_copy(n, e).start()

    def cross(n, e):
        @pl.when(depth == 0)
        def _():
            cross_copy(n, e).start()

    def to_middle(n, e):
        for here in range(1, half):
            @pl.when(depth == here)
            def _():
                relay_copy(n, here, e).start()

    relayed = set()

    def forward(n, e):
        kind = units[n][0]
        first = (kind, e) not in relayed
        relayed.add((kind, e))
        for far in range(1, half):
            @pl.when(depth == 0)
            def _():
                if first:
                    whole = relay_buf.at[far - 1, e, pl.ds(KINDS.index(kind) * capacity * rows, capacity * rows)]
                    z_copy(whole, whole, 0, relay_id(kind, far, e), my_group).wait_recv()
                forward_copy(n, far, e).start()

    def arrive(buf, in_id):
        others = buf.at[pl.ds(0, groups - 1)]
        z_copy(others, others, 0, in_id, my_group).wait_recv()

    def sent():
        whole = send_buf.at[0]
        for e in range(half):
            @pl.when(depth != e)
            def _():
                z_copy(whole, whole, e, 0, my_group).wait_send()
            z_copy(whole, whole, half + e, 0, my_group).wait_send()
        for flow in range(2 * half, half + half * half):
            @pl.when(depth == 0)
            def _():
                z_copy(whole, whole, flow, 0, my_group).wait_send()

    def collect(kind, own_ref):
        n = FIRST_KINDS.index(kind)
        arrive(recv_bufs[n], n)
        for j in range(per_owner):
            own_ref[j * rows:(j + 1) * rows, :] = recv_bufs[n][sources[j], ranks[j]]

    def hear(distance):
        for there, semaphore in ((my_group >= distance, from_low), (my_group + distance < groups, from_high)):
            @pl.when(there)
            def _():
                pl.semaphore_wait(semaphore.at[distance - 2], 1)

    def pass_on(distance):
        tell((my_group >= distance) & has_high, from_low.at[distance - 1], my_group + 1)
        tell((my_group + distance < groups) & has_low, from_high.at[distance - 1], my_group - 1)

    key_units, value_units, query_units = ([n for n, (kind, _) in enumerate(units) if kind == want] for want in FIRST_KINDS)
    update_units = list(range(3 * capacity, len(units)))
    pairs = key_units + value_units
    far_first = list(range(half - 1, -1, -1))
    query_order = [(n, e) for e in far_first for n in query_units]
    ends_at = [(chunks[c][0] + (chunks[c][1] + chunks[c][2]) / rows) / capacity for c in range(len(chunks))]
    update_order = sorted(
        ((n, e) for n in update_units for e in far_first),
        key=lambda one: ends_at[one[0] - update_units[0]] * SPREAD[one[1] > 0][0] + SPREAD[one[1] > 0][1])

    ingest_copy.wait()
    fill(KEY, 0)
    pl.semaphore_wait(barrier, neighbours + ctxs + heads - 2)
    for n in pairs:
        if n > 0:
            fill(*units[n])
        if n == 1:
            for distance in range(1, half):
                if distance > 1:
                    hear(distance)
                pass_on(distance)
        cross(n, 0)
        to_middle(n, 0)
        side(n, True)
    for e in range(1, half):
        for n in pairs:
            to_middle(n, e)
    for n in pairs:
        side(n, False)
    for n in query_units:
        fill(QUERY, units[n][1])
        side(n, True)
    for k in range(capacity):
        fill(UPDATE, k)
    for n in update_units:
        side(n, True)
    for group, sequence in ((query_units, query_order), (update_units, update_order)):
        for n, e in sequence:
            to_middle(n, e)
        for n in group:
            side(n, False)
    for kind in KINDS:
        keep(kind)
    if half > 1:
        hear(half)
    for n in pairs:
        forward(n, 0)
    for e in range(1, half):
        for group in (key_units, value_units):
            for n in group:
                cross(n, e)
            for n in group:
                forward(n, e)

    w_copies = []
    for offset in range(1, heads):
        to = lax.rem(my_head + offset, heads)
        copy = pltpu.make_async_remote_copy(
            src_ref=w_ref.at[:, pl.ds(pl.multiple_of(to * HD, HD), HD)], dst_ref=w_cols.at[my_head],
            send_sem=w_send.at[offset - 1], recv_sem=w_recv,
            device_id={"head": to}, device_id_type=MESH)
        copy.start()
        w_copies.append(copy)
    w_cols[my_head] = w_ref[:, pl.ds(pl.multiple_of(my_head * HD, HD), HD)]

    ends, total = [], jnp.int32(0)
    for u in range(hist_ref.shape[0]):
        total = total + hist_ref[u]
        ends.append(total)
    base = my_ctx * row_count
    position = base + lax.broadcasted_iota(jnp.int32, (row_count, HD), 0)
    first = jnp.zeros((row_count, HD), jnp.int32)
    for end in ends:
        first = jnp.where(position >= end, end, first)
    start_ref[...] = first - base

    def ctx_copy(n, own_ref, prev_ref, offset):
        return pltpu.make_async_remote_copy(
            src_ref=own_ref, dst_ref=prev_ref.at[offset - 1],
            send_sem=c_send.at[n, offset - 1], recv_sem=c_recv.at[n, offset - 1],
            device_id={"ctx": lax.rem(my_ctx + offset, ctxs)}, device_id_type=MESH)

    def push(n, own_ref, prev_ref):
        for offset in range(1, window + 1):
            @pl.when(my_ctx + offset < ctxs)
            def _():
                ctx_copy(n, own_ref, prev_ref, offset).start()

    collect(KEY, own_k)
    push(0, own_k, prev_k)
    collect(VALUE, own_v)
    push(1, own_v, prev_v)
    for n, e in query_order + update_order:
        cross(n, e)
        forward(n, e)
    collect(QUERY, own_q)

    tile = 2 * rows if per_owner % 2 == 0 else rows
    tiles = row_count // tile
    half_scale = 0.5 / math.sqrt(HD)

    def attend(q, key_tile, value_tile, q_lo, k_lo, shift, causal):
        scores = lax.dot_general(q, key_tile, (((1,), (1,)), ((), ())), preferred_element_type=jnp.float32)
        half = scores * half_scale
        act = half + half * jnp.tanh(half)
        key_pos = lax.broadcasted_iota(jnp.int32, (tile, tile), 1) + (k_lo - shift)
        first_pos = jnp.concatenate([start_ref[q_lo:q_lo + tile, :]] * (tile // HD), axis=1)
        visible = key_pos >= first_pos
        if causal:
            visible = visible & (key_pos <= lax.broadcasted_iota(jnp.int32, (tile, tile), 0) + q_lo)
        weights = jnp.where(visible, act, 0.0).astype(jnp.bfloat16)
        return jnp.dot(weights, value_tile, preferred_element_type=jnp.float32)

    def put(i, value, add):
        for part in range(tile // rows):
            at = i * (tile // rows) + part
            piece = value[part * rows:(part + 1) * rows]
            att[at] = att[at] + piece if add else piece

    for i in range(tiles):
        q = own_q[i * tile:(i + 1) * tile, :]
        acc = None
        for t in range(i + 1):
            span = slice(t * tile, (t + 1) * tile)
            term = attend(q, own_k[span, :], own_v[span, :], i * tile, t * tile, 0, t == i)
            acc = term if acc is None else acc + term
        put(i, acc, False)
    for offset in range(1, window + 1):
        @pl.when(my_ctx >= offset)
        def _():
            ctx_copy(0, own_k, prev_k, offset).wait_recv()
            ctx_copy(1, own_v, prev_v, offset).wait_recv()
            for i in range(tiles):
                q = own_q[i * tile:(i + 1) * tile, :]
                acc = None
                for t in range(i if offset == window else 0, tiles):
                    span = slice(t * tile, (t + 1) * tile)
                    term = attend(q, prev_k[offset - 1, span, :], prev_v[offset - 1, span, :],
                                  i * tile, t * tile, offset * row_count, False)
                    acc = term if acc is None else acc + term
                put(i, acc, True)

    source_other = sources[0]
    for j in range(1, per_owner):
        source_other = jnp.where(sides[j] == 1, sources[j], source_other)
    side_source = (sources[0], source_other)
    for c, (k, low, size) in enumerate(chunks):
        arrive(recv_u[c], 3 + c)
        for part in range(2):
            at = jnp.int32(0)
            for j in range(per_owner):
                at = jnp.where((ranks[j] == k) & (sides[j] == part), j, at)
            rows_f32 = att[at, low:low + size, :]
            mean_square = jnp.mean(rows_f32 * rows_f32, axis=-1, keepdims=True)
            normed = rows_f32 * lax.rsqrt(mean_square + 1e-06)
            update = recv_u[c][side_source[part]].astype(jnp.float32)
            gated[c][my_head, part * size:(part + 1) * size, :] = (normed * update).astype(jnp.bfloat16)
        for offset in range(1, heads):
            copy = pltpu.make_async_remote_copy(
                src_ref=gated[c].at[my_head], dst_ref=gated[c].at[my_head],
                send_sem=h_send.at[offset - 1], recv_sem=h_recv.at[c],
                device_id={"head": lax.rem(my_head + offset, heads)}, device_id_type=MESH)
            copy.start()
    for copy in w_copies:
        copy.wait_send()
    if heads > 1:
        all_cols = w_cols.at[pl.ds(0, heads - 1)]
        pltpu.make_async_copy(all_cols, all_cols, w_recv).wait()
    sent()
    for c, (k, low, size) in enumerate(chunks):
        if heads > 1:
            theirs = gated[c].at[pl.ds(0, heads - 1)]
            pltpu.make_async_copy(theirs, theirs, h_recv.at[c]).wait()
        acc = None
        for h in range(heads):
            term = jnp.dot(gated[c][h], w_cols[h], preferred_element_type=jnp.float32)
            acc = term if acc is None else acc + term
        acc = acc.astype(jnp.bfloat16)
        for side in range(2):
            mixed[2 * k + side, low:low + size, :] = acc[side * size:(side + 1) * size]
    for offset in range(1, heads):
        pltpu.make_async_remote_copy(
            src_ref=own_q, dst_ref=own_q, send_sem=h_send.at[offset - 1], recv_sem=h_recv.at[0],
            device_id={"head": my_head}, device_id_type=MESH).wait_send()
    for j in range(per_owner):
        out_ref[j * rows:(j + 1) * rows, :] = mixed[2 * ranks[j] + sides[j]]
    for offset in range(1, window + 1):
        @pl.when(my_ctx + offset < ctxs)
        def _():
            ctx_copy(0, own_k, prev_k, offset).wait_send()
            ctx_copy(1, own_v, prev_v, offset).wait_send()


def body(ingest, src_shard, src_slot, hist_len, w_out):
    groups, ctxs, heads = (lax.axis_size(a) for a in ("batch", "ctx", "head"))
    slot_total, rows, kinds, width = ingest.shape[2:]
    per_owner = src_shard.shape[2]
    capacity = per_owner // 2
    chunks = update_chunks(capacity, rows)
    half = groups // 2
    spans = max(half - 1, 1)
    window = ctxs // 2
    row_count = per_owner * rows
    bf16 = jnp.bfloat16
    dma = pltpu.SemaphoreType.DMA
    vmem = pl.BlockSpec(memory_space=pltpu.VMEM)
    mixed = pl.pallas_call(
        functools.partial(kernel, (groups, ctxs, heads, per_owner, rows)),
        out_shape=pltpu.VMEM((row_count, width), bf16),
        in_specs=[pl.BlockSpec(memory_space=pl.ANY)] * 5,
        out_specs=vmem,
        scratch_shapes=[
            pltpu.SMEM(src_shard.shape[1:], jnp.int32), pltpu.SMEM(src_slot.shape[1:], jnp.int32),
            pltpu.SMEM(hist_len.shape[1:], jnp.int32), pltpu.VMEM(w_out.shape, bf16), dma((4,)),
            pltpu.VMEM((slot_total, rows * kinds, width), bf16),
            pltpu.VMEM((groups, 4 * capacity * rows, width), bf16),
            [pltpu.VMEM((groups, capacity, rows, width), bf16)] * 3,
            [pltpu.VMEM((groups, size, width), bf16) for _, _, size in chunks],
            pltpu.VMEM((spans, half, 4 * capacity * rows, width), bf16),
            pltpu.VMEM((row_count, width), bf16),
            pltpu.VMEM((row_count, width), bf16),
            pltpu.VMEM((row_count, width), bf16),
            pltpu.VMEM((window, row_count, width), bf16),
            pltpu.VMEM((window, row_count, width), bf16),
            pltpu.VMEM((row_count, width), jnp.int32),
            pltpu.VMEM((per_owner, rows, width), jnp.float32),
            [pltpu.VMEM((heads, 2 * size, width), bf16) for _, _, size in chunks],
            pltpu.VMEM((heads, width, width), bf16),
            pltpu.VMEM((per_owner, rows, width), bf16),
            dma((groups + spans * half,)), dma((3 + len(chunks) + 4 * spans * half,)),
            dma((2, window)), dma((2, window)),
            dma((max(heads - 1, 1),)), dma((len(chunks),)),
            dma((max(heads - 1, 1),)), dma,
            dma, pltpu.SemaphoreType.REGULAR((spans,)), pltpu.SemaphoreType.REGULAR((spans,)),
        ],
        compiler_params=pltpu.CompilerParams(
            collective_id=0, has_side_effects=True, vmem_limit_bytes=56 * 1024 * 1024),
    )(src_shard[0], src_slot[0], hist_len[0],
      ingest.reshape(slot_total, rows * kinds, width), w_out)
    return mixed[None]


def solution(mesh):
    in_specs = (
        P("ctx", "batch", None, None, None, "head"),
        P("ctx", None, None),
        P("ctx", None, None),
        P("batch", None),
        P("head", None),
    )
    out_specs = P("batch", "ctx", "head")
    return jax.shard_map(body, mesh=mesh, in_specs=in_specs, out_specs=out_specs, check_vma=False)
```

```python
import functools
import math

import jax
import jax.numpy as jnp
from jax import lax
from jax.experimental import pallas as pl
from jax.experimental.pallas import tpu as pltpu
from jax.sharding import PartitionSpec as P

HD = 128
MESH = pl.DeviceIdType.MESH
QUERY, KEY, VALUE, UPDATE = 0, 1, 2, 3
FIRST_KINDS = (KEY, VALUE, QUERY)
KINDS = (*FIRST_KINDS, UPDATE)
SPREAD = ((9,3),(8,0))


def unit_list(capacity, rows):
    units = [(kind, k) for kind in FIRST_KINDS for k in range(capacity)]
    return units + [(UPDATE, c) for c in range(len(update_chunks(capacity, rows)))]


def update_chunks(capacity, rows):
    chunks, low = [(k, 0, rows) for k in range(capacity - 1)], 0
    for share in (2,4,4):
        chunks.append((capacity - 1, low, rows // share))
        low += rows // share
    return chunks


def kernel(sizes, shard_hbm, slot_hbm, hist_hbm, ingest_hbm, w_hbm, out_ref,
           shard_ref, slot_ref, hist_ref, w_ref, local_sems,
           ingest_ref,
           send_buf, recv_bufs, recv_u, relay_buf, own_k, own_v, own_q, prev_k, prev_v,
           start_ref, att, gated, w_cols, mixed,
           z_send, z_recv, c_send, c_recv, h_send, h_recv, w_send, w_recv,
           ingest_sem, from_low, from_high):
    groups, ctxs, heads, per_owner, rows = sizes
    capacity = per_owner // 2
    chunks = update_chunks(capacity, rows)
    window = ctxs // 2
    row_count = per_owner * rows
    my_group = lax.axis_index("batch")
    my_ctx = lax.axis_index("ctx")
    my_head = lax.axis_index("head")

    barrier = pltpu.get_barrier_semaphore()
    ingest_copy = pltpu.make_async_copy(ingest_hbm, ingest_ref, ingest_sem)
    ingest_copy.start()
    local_copies = [pltpu.make_async_copy(src, dst, local_sems.at[i]) for i, (src, dst) in enumerate((
        (shard_hbm, shard_ref), (slot_hbm, slot_ref), (hist_hbm, hist_ref), (w_hbm, w_ref)))]
    for copy in local_copies:
        copy.start()
    for axis, me, count in (("ctx", my_ctx, ctxs), ("head", my_head, heads)):
        for offset in range(1, count):
            pl.semaphore_signal(barrier, inc=1, device_id={axis: lax.rem(me + offset, count)}, device_id_type=MESH)
    has_low, has_high = my_group > 0, my_group < groups - 1

    def tell(there, semaphore, to):
        @pl.when(there)
        def _():
            pl.semaphore_signal(semaphore, inc=1, device_id={"batch": to}, device_id_type=MESH)

    tell(has_low, barrier, my_group - 1)
    tell(has_high, barrier, my_group + 1)
    neighbours = jnp.where(has_low, 1, 0) + jnp.where(has_high, 1, 0)

    for copy in local_copies:
        copy.wait()
    slots = []
    for dst in range(groups):
        picked = [jnp.int32(0)] * capacity
        seen = jnp.int32(0)
        for j in range(per_owner):
            hit = shard_ref[dst, j] == my_group
            slot = slot_ref[dst, j]
            for k in range(capacity):
                picked[k] = jnp.where(hit & (seen == k), slot, picked[k])
            seen = seen + jnp.where(hit, 1, 0)
        slots.append(picked)

    sources = [shard_ref[my_group, j] for j in range(per_owner)]
    ranks, sides = [], []
    for j in range(per_owner):
        rank = jnp.int32(0)
        for i in range(j):
            rank = rank + jnp.where(sources[i] == sources[j], 1, 0)
        ranks.append(jnp.minimum(rank, capacity - 1))
        sides.append(jnp.where(sources[j] == sources[0], 0, 1))

    def split_kind(kind):
        width = 4 * rows
        row = lax.broadcasted_iota(jnp.int32, (rows, width), 0)
        col = lax.broadcasted_iota(jnp.int32, (rows, width), 1)
        pick = jnp.where(col == row * 4 + kind, 1.0, 0.0).astype(jnp.bfloat16)

        def one(dst, k):
            block = ingest_ref[slots[dst][k]]
            return jnp.dot(pick, block, preferred_element_type=jnp.float32).astype(jnp.bfloat16)

        return one

    units = unit_list(capacity, rows)
    half = groups // 2
    low_side = my_group < half
    depth = jnp.where(low_side, half - 1 - my_group, my_group - half)

    def same(e):
        return jnp.where(low_side, half - 1 - e, half + e)

    def other(e):
        return jnp.where(low_side, half + e, half - 1 - e)

    def fill(kind, k):
        one = split_kind(kind)
        low = (KINDS.index(kind) * capacity + k) * rows
        for dst in range(groups):
            send_buf[dst, low:low + rows, :] = one(dst, k)

    def span(n):
        kind, c = units[n]
        k, low, size = chunks[c] if kind == UPDATE else (c, 0, rows)
        return pl.ds((KINDS.index(kind) * capacity + k) * rows + low, size)

    def inbox(n, src):
        kind, c = units[n]
        return recv_u[c].at[src] if kind == UPDATE else recv_bufs[FIRST_KINDS.index(kind)].at[src, c]

    def keep(kind):
        for n, (of, _) in enumerate(units):
            if of == kind:
                inbox(n, my_group)[...] = send_buf[my_group, span(n), :]

    def z_copy(src, dst, out_id, in_id, to):
        return pltpu.make_async_remote_copy(
            src_ref=src, dst_ref=dst, send_sem=z_send.at[out_id], recv_sem=z_recv.at[in_id],
            device_id={"batch": to}, device_id_type=MESH)

    def here_id(n):
        kind, c = units[n]
        return 3 + c if kind == UPDATE else FIRST_KINDS.index(kind)

    def relay_id(kind, far, e):
        return 3 + len(chunks) + (KINDS.index(kind) * (half - 1) + far - 1) * half + e

    def side_copy(n, e):
        return z_copy(send_buf.at[same(e), span(n)], inbox(n, my_group), e, here_id(n), same(e))

    def cross_copy(n, e):
        return z_copy(send_buf.at[other(e), span(n)], inbox(n, my_group), half + e, here_id(n), other(e))

    def relay_copy(n, far, e):
        return z_copy(send_buf.at[other(e), span(n)], relay_buf.at[far - 1, e, span(n)],
                      half + e, relay_id(units[n][0], far, e), same(0))

    def forward_copy(n, far, e):
        return z_copy(relay_buf.at[far - 1, e, span(n)], inbox(n, same(far)),
                      2 * half + (far - 1) * half + e, here_id(n), other(e))

    def side(n, middle):
        for here in range(half):
            if (here == 0) == middle and half > 1:
                @pl.when(depth == here)
                def _():
                    for e in range(half):
                        if e != here:
                            side_copy(n, e).start()

    def cross(n, e):
        @pl.when(depth == 0)
        def _():
            cross_copy(n, e).start()

    def to_middle(n, e):
        for here in range(1, half):
            @pl.when(depth == here)
            def _():
                relay_copy(n, here, e).start()

    relayed = set()

    def forward(n, e):
        kind = units[n][0]
        first = (kind, e) not in relayed
        relayed.add((kind, e))
        for far in range(1, half):
            @pl.when(depth == 0)
            def _():
                if first:
                    whole = relay_buf.at[far - 1, e, pl.ds(KINDS.index(kind) * capacity * rows, capacity * rows)]
                    z_copy(whole, whole, 0, relay_id(kind, far, e), my_group).wait_recv()
                forward_copy(n, far, e).start()

    def arrive(buf, in_id):
        others = buf.at[pl.ds(0, groups - 1)]
        z_copy(others, others, 0, in_id, my_group).wait_recv()

    def sent():
        whole = send_buf.at[0]
        for e in range(half):
            @pl.when(depth != e)
            def _():
                z_copy(whole, whole, e, 0, my_group).wait_send()
            z_copy(whole, whole, half + e, 0, my_group).wait_send()
        for flow in range(2 * half, half + half * half):
            @pl.when(depth == 0)
            def _():
                z_copy(whole, whole, flow, 0, my_group).wait_send()

    def collect(kind, own_ref):
        n = FIRST_KINDS.index(kind)
        arrive(recv_bufs[n], n)
        for j in range(per_owner):
            own_ref[j * rows:(j + 1) * rows, :] = recv_bufs[n][sources[j], ranks[j]]

    def hear(distance):
        for there, semaphore in ((my_group >= distance, from_low), (my_group + distance < groups, from_high)):
            @pl.when(there)
            def _():
                pl.semaphore_wait(semaphore.at[distance - 2], 1)

    def pass_on(distance):
        tell((my_group >= distance) & has_high, from_low.at[distance - 1], my_group + 1)
        tell((my_group + distance < groups) & has_low, from_high.at[distance - 1], my_group - 1)

    key_units, value_units, query_units = ([n for n, (kind, _) in enumerate(units) if kind == want] for want in FIRST_KINDS)
    update_units = list(range(3 * capacity, len(units)))
    pairs = key_units + value_units
    far_first = list(range(half - 1, -1, -1))
    early = [(n, 0) for n in query_units]
    query_order = [(n, e) for e in far_first for n in query_units]
    ends_at = [(chunks[c][0] + (chunks[c][1] + chunks[c][2]) / rows) / capacity for c in range(len(chunks))]
    update_order = sorted(
        ((n, e) for n in update_units for e in far_first),
        key=lambda one: ends_at[one[0] - update_units[0]] * SPREAD[one[1] > 0][0] + SPREAD[one[1] > 0][1])

    ingest_copy.wait()
    fill(KEY, 0)
    pl.semaphore_wait(barrier, neighbours + ctxs + heads - 2)
    for n in pairs:
        if n > 0:
            fill(*units[n])
        if n == 1:
            for distance in range(1, half):
                if distance > 1:
                    hear(distance)
                pass_on(distance)
        cross(n, 0)
        to_middle(n, 0)
        side(n, True)
    for e in range(1, half):
        for n in pairs:
            to_middle(n, e)
    for n in pairs:
        side(n, False)
    for n in query_units:
        fill(QUERY, units[n][1])
        cross(n, 0)
        side(n, True)
    for k in range(capacity):
        fill(UPDATE, k)
    for n in update_units:
        side(n, True)
    for group, sequence in ((query_units, query_order), (update_units, update_order)):
        for n, e in sequence:
            to_middle(n, e)
        for n in group:
            side(n, False)
    for kind in KINDS:
        keep(kind)
    if half > 1:
        hear(half)
    for n in pairs:
        forward(n, 0)
    for e in range(1, half):
        for group in (key_units, value_units):
            for n in group:
                cross(n, e)
            for n in group:
                forward(n, e)

    w_copies = []
    for offset in range(1, heads):
        to = lax.rem(my_head + offset, heads)
        copy = pltpu.make_async_remote_copy(
            src_ref=w_ref.at[:, pl.ds(pl.multiple_of(to * HD, HD), HD)], dst_ref=w_cols.at[my_head],
            send_sem=w_send.at[offset - 1], recv_sem=w_recv,
            device_id={"head": to}, device_id_type=MESH)
        copy.start()
        w_copies.append(copy)
    w_cols[my_head] = w_ref[:, pl.ds(pl.multiple_of(my_head * HD, HD), HD)]

    ends, total = [], jnp.int32(0)
    for u in range(hist_ref.shape[0]):
        total = total + hist_ref[u]
        ends.append(total)
    base = my_ctx * row_count
    position = base + lax.broadcasted_iota(jnp.int32, (row_count, HD), 0)
    first = jnp.zeros((row_count, HD), jnp.int32)
    for end in ends:
        first = jnp.where(position >= end, end, first)
    start_ref[...] = first - base

    def ctx_copy(n, own_ref, prev_ref, offset):
        return pltpu.make_async_remote_copy(
            src_ref=own_ref, dst_ref=prev_ref.at[offset - 1],
            send_sem=c_send.at[n, offset - 1], recv_sem=c_recv.at[n, offset - 1],
            device_id={"ctx": lax.rem(my_ctx + offset, ctxs)}, device_id_type=MESH)

    def push(n, own_ref, prev_ref):
        for offset in range(1, window + 1):
            @pl.when(my_ctx + offset < ctxs)
            def _():
                ctx_copy(n, own_ref, prev_ref, offset).start()

    collect(KEY, own_k)
    push(0, own_k, prev_k)
    collect(VALUE, own_v)
    push(1, own_v, prev_v)
    for n, e in query_order + update_order:
        if (n, e) not in early:
            cross(n, e)
        forward(n, e)
    collect(QUERY, own_q)

    tile = 2 * rows if per_owner % 2 == 0 else rows
    tiles = row_count // tile
    half_scale = 0.5 / math.sqrt(HD)

    def attend(q, key_tile, value_tile, q_lo, k_lo, shift, causal):
        scores = lax.dot_general(q, key_tile, (((1,), (1,)), ((), ())), preferred_element_type=jnp.float32)
        half = scores * half_scale
        act = half + half * jnp.tanh(half)
        key_pos = lax.broadcasted_iota(jnp.int32, (tile, tile), 1) + (k_lo - shift)
        first_pos = jnp.concatenate([start_ref[q_lo:q_lo + tile, :]] * (tile // HD), axis=1)
        visible = key_pos >= first_pos
        if causal:
            visible = visible & (key_pos <= lax.broadcasted_iota(jnp.int32, (tile, tile), 0) + q_lo)
        weights = jnp.where(visible, act, 0.0).astype(jnp.bfloat16)
        return jnp.dot(weights, value_tile, preferred_element_type=jnp.float32)

    def put(i, value, add):
        for part in range(tile // rows):
            at = i * (tile // rows) + part
            piece = value[part * rows:(part + 1) * rows]
            att[at] = att[at] + piece if add else piece

    for i in range(tiles):
        q = own_q[i * tile:(i + 1) * tile, :]
        acc = None
        for t in range(i + 1):
            span = slice(t * tile, (t + 1) * tile)
            term = attend(q, own_k[span, :], own_v[span, :], i * tile, t * tile, 0, t == i)
            acc = term if acc is None else acc + term
        put(i, acc, False)
    for offset in range(1, window + 1):
        @pl.when(my_ctx >= offset)
        def _():
            ctx_copy(0, own_k, prev_k, offset).wait_recv()
            ctx_copy(1, own_v, prev_v, offset).wait_recv()
            for i in range(tiles):
                q = own_q[i * tile:(i + 1) * tile, :]
                acc = None
                for t in range(i if offset == window else 0, tiles):
                    span = slice(t * tile, (t + 1) * tile)
                    term = attend(q, prev_k[offset - 1, span, :], prev_v[offset - 1, span, :],
                                  i * tile, t * tile, offset * row_count, False)
                    acc = term if acc is None else acc + term
                put(i, acc, True)

    source_other = sources[0]
    for j in range(1, per_owner):
        source_other = jnp.where(sides[j] == 1, sources[j], source_other)
    side_source = (sources[0], source_other)
    for c, (k, low, size) in enumerate(chunks):
        arrive(recv_u[c], 3 + c)
        for part in range(2):
            at = jnp.int32(0)
            for j in range(per_owner):
                at = jnp.where((ranks[j] == k) & (sides[j] == part), j, at)
            rows_f32 = att[at, low:low + size, :]
            mean_square = jnp.mean(rows_f32 * rows_f32, axis=-1, keepdims=True)
            normed = rows_f32 * lax.rsqrt(mean_square + 1e-06)
            update = recv_u[c][side_source[part]].astype(jnp.float32)
            gated[c][my_head, part * size:(part + 1) * size, :] = (normed * update).astype(jnp.bfloat16)
        for offset in range(1, heads):
            copy = pltpu.make_async_remote_copy(
                src_ref=gated[c].at[my_head], dst_ref=gated[c].at[my_head],
                send_sem=h_send.at[offset - 1], recv_sem=h_recv.at[c],
                device_id={"head": lax.rem(my_head + offset, heads)}, device_id_type=MESH)
            copy.start()
    for copy in w_copies:
        copy.wait_send()
    if heads > 1:
        all_cols = w_cols.at[pl.ds(0, heads - 1)]
        pltpu.make_async_copy(all_cols, all_cols, w_recv).wait()
    sent()
    for c, (k, low, size) in enumerate(chunks):
        if heads > 1:
            theirs = gated[c].at[pl.ds(0, heads - 1)]
            pltpu.make_async_copy(theirs, theirs, h_recv.at[c]).wait()
        acc = None
        for h in range(heads):
            term = jnp.dot(gated[c][h], w_cols[h], preferred_element_type=jnp.float32)
            acc = term if acc is None else acc + term
        acc = acc.astype(jnp.bfloat16)
        for side in range(2):
            mixed[2 * k + side, low:low + size, :] = acc[side * size:(side + 1) * size]
    for offset in range(1, heads):
        pltpu.make_async_remote_copy(
            src_ref=own_q, dst_ref=own_q, send_sem=h_send.at[offset - 1], recv_sem=h_recv.at[0],
            device_id={"head": my_head}, device_id_type=MESH).wait_send()
    for j in range(per_owner):
        out_ref[j * rows:(j + 1) * rows, :] = mixed[2 * ranks[j] + sides[j]]
    for offset in range(1, window + 1):
        @pl.when(my_ctx + offset < ctxs)
        def _():
            ctx_copy(0, own_k, prev_k, offset).wait_send()
            ctx_copy(1, own_v, prev_v, offset).wait_send()


def body(ingest, src_shard, src_slot, hist_len, w_out):
    groups, ctxs, heads = (lax.axis_size(a) for a in ("batch", "ctx", "head"))
    slot_total, rows, kinds, width = ingest.shape[2:]
    per_owner = src_shard.shape[2]
    capacity = per_owner // 2
    chunks = update_chunks(capacity, rows)
    half = groups // 2
    spans = max(half - 1, 1)
    window = ctxs // 2
    row_count = per_owner * rows
    bf16 = jnp.bfloat16
    dma = pltpu.SemaphoreType.DMA
    vmem = pl.BlockSpec(memory_space=pltpu.VMEM)
    mixed = pl.pallas_call(
        functools.partial(kernel, (groups, ctxs, heads, per_owner, rows)),
        out_shape=pltpu.VMEM((row_count, width), bf16),
        in_specs=[pl.BlockSpec(memory_space=pl.ANY)] * 5,
        out_specs=vmem,
        scratch_shapes=[
            pltpu.SMEM(src_shard.shape[1:], jnp.int32), pltpu.SMEM(src_slot.shape[1:], jnp.int32),
            pltpu.SMEM(hist_len.shape[1:], jnp.int32), pltpu.VMEM(w_out.shape, bf16), dma((4,)),
            pltpu.VMEM((slot_total, rows * kinds, width), bf16),
            pltpu.VMEM((groups, 4 * capacity * rows, width), bf16),
            [pltpu.VMEM((groups, capacity, rows, width), bf16)] * 3,
            [pltpu.VMEM((groups, size, width), bf16) for _, _, size in chunks],
            pltpu.VMEM((spans, half, 4 * capacity * rows, width), bf16),
            pltpu.VMEM((row_count, width), bf16),
            pltpu.VMEM((row_count, width), bf16),
            pltpu.VMEM((row_count, width), bf16),
            pltpu.VMEM((window, row_count, width), bf16),
            pltpu.VMEM((window, row_count, width), bf16),
            pltpu.VMEM((row_count, width), jnp.int32),
            pltpu.VMEM((per_owner, rows, width), jnp.float32),
            [pltpu.VMEM((heads, 2 * size, width), bf16) for _, _, size in chunks],
            pltpu.VMEM((heads, width, width), bf16),
            pltpu.VMEM((per_owner, rows, width), bf16),
            dma((groups + spans * half,)), dma((3 + len(chunks) + 4 * spans * half,)),
            dma((2, window)), dma((2, window)),
            dma((max(heads - 1, 1),)), dma((len(chunks),)),
            dma((max(heads - 1, 1),)), dma,
            dma, pltpu.SemaphoreType.REGULAR((spans,)), pltpu.SemaphoreType.REGULAR((spans,)),
        ],
        compiler_params=pltpu.CompilerParams(
            collective_id=0, has_side_effects=True, vmem_limit_bytes=56 * 1024 * 1024),
    )(src_shard[0], src_slot[0], hist_len[0],
      ingest.reshape(slot_total, rows * kinds, width), w_out)
    return mixed[None]


def solution(mesh):
    in_specs = (
        P("ctx", "batch", None, None, None, "head"),
        P("ctx", None, None),
        P("ctx", None, None),
        P("batch", None),
        P("head", None),
    )
    out_specs = P("batch", "ctx", "head")
    return jax.shard_map(body, mesh=mesh, in_specs=in_specs, out_specs=out_specs, check_vma=False)
```

```python
import functools
import math

import jax
import jax.numpy as jnp
from jax import lax
from jax.experimental import pallas as pl
from jax.experimental.pallas import tpu as pltpu
from jax.sharding import PartitionSpec as P

HD = 128
MESH = pl.DeviceIdType.MESH
QUERY, KEY, VALUE, UPDATE = 0, 1, 2, 3
FIRST_KINDS = (KEY, VALUE, QUERY)
KINDS = (*FIRST_KINDS, UPDATE)
SPREAD = ((9,3),(7,0))
NEAR_QUERY = -0.5
NEAR_FIRST = 2.4
SPLITS = ((1,),(2,2),(2,4,4))


def load_pieces(rows):
    return [(0, rows // 4), (rows // 4, rows - rows // 4)]


def unit_list(capacity, rows):
    units = [(KEY, 0, 0, low, size) for low, size in load_pieces(rows)]
    units += [(KEY, k, k, 0, rows) for k in range(1, capacity)]
    units += [(kind, k, k, 0, rows) for kind in FIRST_KINDS[1:] for k in range(capacity)]
    return units + [(UPDATE, c, *chunk) for c, chunk in enumerate(update_chunks(capacity, rows))]


def update_chunks(capacity, rows):
    chunks = []
    for k in range(capacity):
        low = 0
        for share in SPLITS[max(k + len(SPLITS) - capacity, 0)]:
            chunks.append((k, low, rows // share))
            low += rows // share
    return chunks


def kernel(sizes, shard_hbm, slot_hbm, hist_hbm, ingest_hbm, w_hbm, out_ref,
           shard_ref, slot_ref, hist_ref, w_ref, local_sems,
           ingest_refs,
           send_buf, recv_bufs, recv_u, relay_buf, own_k, own_v, own_q, prev_k, prev_v,
           start_ref, att, gated, w_cols, mixed,
           z_send, z_recv, c_send, c_recv, h_send, h_recv, w_send, w_recv,
           ingest_sems, from_low, from_high):
    groups, ctxs, heads, per_owner, rows = sizes
    capacity = per_owner // 2
    chunks = update_chunks(capacity, rows)
    window = ctxs // 2
    row_count = per_owner * rows
    my_group = lax.axis_index("batch")
    my_ctx = lax.axis_index("ctx")
    my_head = lax.axis_index("head")

    barrier = pltpu.get_barrier_semaphore()
    local_copies = [pltpu.make_async_copy(src, dst, local_sems.at[i]) for i, (src, dst) in enumerate((
        (shard_hbm, shard_ref), (slot_hbm, slot_ref), (hist_hbm, hist_ref), (w_hbm, w_ref)))]
    pieces = load_pieces(rows)
    kinds = ingest_hbm.shape[1] // rows
    ingest_copies = [pltpu.make_async_copy(
        ingest_hbm.at[:, pl.ds(low * kinds, size * kinds), :], ingest_refs[p], ingest_sems.at[p])
        for p, (low, size) in enumerate(pieces)]
    for copy in (*local_copies[:2], *ingest_copies, *local_copies[2:]):
        copy.start()
    for axis, me, count in (("ctx", my_ctx, ctxs), ("head", my_head, heads)):
        for offset in range(1, count):
            pl.semaphore_signal(barrier, inc=1, device_id={axis: lax.rem(me + offset, count)}, device_id_type=MESH)
    has_low, has_high = my_group > 0, my_group < groups - 1

    def tell(there, semaphore, to):
        @pl.when(there)
        def _():
            pl.semaphore_signal(semaphore, inc=1, device_id={"batch": to}, device_id_type=MESH)

    tell(has_low, barrier, my_group - 1)
    tell(has_high, barrier, my_group + 1)
    neighbours = jnp.where(has_low, 1, 0) + jnp.where(has_high, 1, 0)

    for copy in local_copies[:2]:
        copy.wait()
    slots = []
    for dst in range(groups):
        picked = [jnp.int32(0)] * capacity
        seen = jnp.int32(0)
        for j in range(per_owner):
            hit = shard_ref[dst, j] == my_group
            slot = slot_ref[dst, j]
            for k in range(capacity):
                picked[k] = jnp.where(hit & (seen == k), slot, picked[k])
            seen = seen + jnp.where(hit, 1, 0)
        slots.append(picked)

    sources = [shard_ref[my_group, j] for j in range(per_owner)]
    ranks, sides = [], []
    for j in range(per_owner):
        rank = jnp.int32(0)
        for i in range(j):
            rank = rank + jnp.where(sources[i] == sources[j], 1, 0)
        ranks.append(jnp.minimum(rank, capacity - 1))
        sides.append(jnp.where(sources[j] == sources[0], 0, 1))

    fine = rows // 4

    def split_kind(kind):
        row = lax.broadcasted_iota(jnp.int32, (fine, fine * kinds), 0)
        col = lax.broadcasted_iota(jnp.int32, (fine, fine * kinds), 1)
        pick = jnp.where(col == row * kinds + kind, 1.0, 0.0).astype(jnp.bfloat16)

        def one(dst, k, low):
            p = max(p for p, (first, _) in enumerate(pieces) if first <= low)
            at = (low - pieces[p][0]) * kinds
            block = ingest_refs[p][slots[dst][k], at:at + fine * kinds, :]
            return jnp.dot(pick, block, preferred_element_type=jnp.float32).astype(jnp.bfloat16)

        return one

    units = unit_list(capacity, rows)
    half = groups // 2
    low_side = my_group < half
    depth = jnp.where(low_side, half - 1 - my_group, my_group - half)

    def same(e):
        return jnp.where(low_side, half - 1 - e, half + e)

    def other(e):
        return jnp.where(low_side, half + e, half - 1 - e)

    def fill(kind, k, low, size):
        one = split_kind(kind)
        base = (KINDS.index(kind) * capacity + k) * rows
        for dst in range(groups):
            for at in range(low, low + size, fine):
                send_buf[dst, base + at:base + at + fine, :] = one(dst, k, at)

    def span(n):
        kind, _, k, low, size = units[n]
        return pl.ds((KINDS.index(kind) * capacity + k) * rows + low, size)

    def inbox(n, src):
        kind, c, k, low, size = units[n]
        return recv_u[c].at[src] if kind == UPDATE else recv_bufs[FIRST_KINDS.index(kind)].at[src, k, pl.ds(low, size)]

    def keep(kind):
        for n, unit in enumerate(units):
            if unit[0] == kind:
                inbox(n, my_group)[...] = send_buf[my_group, span(n), :]

    def z_copy(src, dst, out_id, in_id, to):
        return pltpu.make_async_remote_copy(
            src_ref=src, dst_ref=dst, send_sem=z_send.at[out_id], recv_sem=z_recv.at[in_id],
            device_id={"batch": to}, device_id_type=MESH)

    def here_id(n):
        kind, c = units[n][:2]
        return 3 + c if kind == UPDATE else FIRST_KINDS.index(kind)

    def relay_id(kind, far, e):
        return 3 + len(chunks) + (KINDS.index(kind) * (half - 1) + far - 1) * half + e

    def side_copy(n, e):
        return z_copy(send_buf.at[same(e), span(n)], inbox(n, my_group), e, here_id(n), same(e))

    def cross_copy(n, e):
        return z_copy(send_buf.at[other(e), span(n)], inbox(n, my_group), half + e, here_id(n), other(e))

    def relay_copy(n, far, e):
        return z_copy(send_buf.at[other(e), span(n)], relay_buf.at[far - 1, e, span(n)],
                      half + e, relay_id(units[n][0], far, e), same(0))

    def forward_copy(n, far, e):
        return z_copy(relay_buf.at[far - 1, e, span(n)], inbox(n, same(far)),
                      2 * half + (far - 1) * half + e, here_id(n), other(e))

    def side(n, middle):
        for here in range(half):
            if (here == 0) == middle and half > 1:
                @pl.when(depth == here)
                def _():
                    for e in range(half):
                        if e != here:
                            side_copy(n, e).start()

    def cross(n, e):
        @pl.when(depth == 0)
        def _():
            cross_copy(n, e).start()

    def to_middle(n, e):
        for here in range(1, half):
            @pl.when(depth == here)
            def _():
                relay_copy(n, here, e).start()

    relayed = set()

    def forward(n, e):
        kind = units[n][0]
        first = (kind, e) not in relayed
        relayed.add((kind, e))
        for far in range(1, half):
            @pl.when(depth == 0)
            def _():
                if first:
                    whole = relay_buf.at[far - 1, e, pl.ds(KINDS.index(kind) * capacity * rows, capacity * rows)]
                    z_copy(whole, whole, 0, relay_id(kind, far, e), my_group).wait_recv()
                forward_copy(n, far, e).start()

    def arrive(buf, in_id):
        others = buf.at[pl.ds(0, groups - 1)]
        z_copy(others, others, 0, in_id, my_group).wait_recv()

    def sent():
        whole = send_buf.at[0]
        for e in range(half):
            @pl.when(depth != e)
            def _():
                z_copy(whole, whole, e, 0, my_group).wait_send()
            z_copy(whole, whole, half + e, 0, my_group).wait_send()
        for flow in range(2 * half, half + half * half):
            @pl.when(depth == 0)
            def _():
                z_copy(whole, whole, flow, 0, my_group).wait_send()

    def collect(kind, own_ref):
        n = FIRST_KINDS.index(kind)
        arrive(recv_bufs[n], n)
        for j in range(per_owner):
            own_ref[j * rows:(j + 1) * rows, :] = recv_bufs[n][sources[j], ranks[j]]

    def hear(distance):
        for there, semaphore in ((my_group >= distance, from_low), (my_group + distance < groups, from_high)):
            @pl.when(there)
            def _():
                pl.semaphore_wait(semaphore.at[distance - 2], 1)

    def pass_on(distance):
        tell((my_group >= distance) & has_high, from_low.at[distance - 1], my_group + 1)
        tell((my_group + distance < groups) & has_low, from_high.at[distance - 1], my_group - 1)

    key_units, value_units, query_units = ([n for n, unit in enumerate(units) if unit[0] == want] for want in FIRST_KINDS)
    update_units = [n for n, unit in enumerate(units) if unit[0] == UPDATE]
    pairs = key_units + value_units
    far_first = list(range(half - 1, -1, -1))
    early = [(n, 0) for n in query_units]
    ends_at = [(k + (low + size) / rows) / capacity for k, low, size in chunks]

    def turn(one):
        n, e = one
        if n in query_units:
            return NEAR_QUERY if e == 0 else -1
        if (n, e) == (update_units[0], 0):
            return NEAR_FIRST
        slope, first = SPREAD[e > 0]
        return ends_at[n - update_units[0]] * slope + first

    late_order = sorted([(n, e) for n in query_units + update_units for e in far_first], key=turn)

    ingest_copies[0].wait()
    fill(KEY, *units[0][2:])
    pl.semaphore_wait(barrier, neighbours + ctxs + heads - 2)
    for n in pairs:
        if n == 1:
            for copy in ingest_copies[1:]:
                copy.wait()
        if n > 0:
            fill(units[n][0], *units[n][2:])
        if n == 1:
            for distance in range(1, half):
                if distance > 1:
                    hear(distance)
                pass_on(distance)
        cross(n, 0)
        if n in key_units:
            to_middle(n, 0)
        side(n, True)
    for e in range(1, half):
        for n in pairs:
            to_middle(n, e)
    for n in value_units:
        to_middle(n, 0)
    for n in pairs:
        side(n, False)
    for n in query_units:
        fill(QUERY, *units[n][2:])
        cross(n, 0)
        side(n, True)
    for k in range(capacity):
        fill(UPDATE, k, 0, rows)
    for n in update_units:
        side(n, True)
    for n, e in late_order:
        to_middle(n, e)
    for n in query_units + update_units:
        side(n, False)
    for kind in KINDS:
        keep(kind)
    if half > 1:
        hear(half)
    for n in key_units:
        forward(n, 0)
    for e in range(1, half):
        for group in (key_units, value_units):
            for n in group:
                cross(n, e)
            for n in group:
                forward(n, e)
    for n in value_units:
        forward(n, 0)

    for copy in local_copies[2:]:
        copy.wait()
    w_copies = []
    for offset in range(1, heads):
        to = lax.rem(my_head + offset, heads)
        copy = pltpu.make_async_remote_copy(
            src_ref=w_ref.at[:, pl.ds(pl.multiple_of(to * HD, HD), HD)], dst_ref=w_cols.at[my_head],
            send_sem=w_send.at[offset - 1], recv_sem=w_recv,
            device_id={"head": to}, device_id_type=MESH)
        copy.start()
        w_copies.append(copy)
    w_cols[my_head] = w_ref[:, pl.ds(pl.multiple_of(my_head * HD, HD), HD)]

    ends, total = [], jnp.int32(0)
    for u in range(hist_ref.shape[0]):
        total = total + hist_ref[u]
        ends.append(total)
    base = my_ctx * row_count
    position = base + lax.broadcasted_iota(jnp.int32, (row_count, HD), 0)
    first = jnp.zeros((row_count, HD), jnp.int32)
    for end in ends:
        first = jnp.where(position >= end, end, first)
    start_ref[...] = first - base

    def ctx_copy(n, own_ref, prev_ref, offset):
        return pltpu.make_async_remote_copy(
            src_ref=own_ref, dst_ref=prev_ref.at[offset - 1],
            send_sem=c_send.at[n, offset - 1], recv_sem=c_recv.at[n, offset - 1],
            device_id={"ctx": lax.rem(my_ctx + offset, ctxs)}, device_id_type=MESH)

    def push(n, own_ref, prev_ref):
        for offset in range(1, window + 1):
            @pl.when(my_ctx + offset < ctxs)
            def _():
                ctx_copy(n, own_ref, prev_ref, offset).start()

    collect(KEY, own_k)
    push(0, own_k, prev_k)
    for n, e in late_order:
        if n in query_units and e > 0:
            cross(n, e)
            forward(n, e)
    collect(VALUE, own_v)
    push(1, own_v, prev_v)
    for n, e in late_order:
        if n in query_units and e > 0:
            continue
        if (n, e) not in early:
            cross(n, e)
        forward(n, e)
    collect(QUERY, own_q)

    tile = 2 * rows if per_owner % 2 == 0 else rows
    tiles = row_count // tile
    half_scale = 0.5 / math.sqrt(HD)

    def attend(q, key_tile, value_tile, q_lo, k_lo, shift, causal):
        scores = lax.dot_general(q, key_tile, (((1,), (1,)), ((), ())), preferred_element_type=jnp.float32)
        half = scores * half_scale
        act = half + half * jnp.tanh(half)
        key_pos = lax.broadcasted_iota(jnp.int32, (tile, tile), 1) + (k_lo - shift)
        first_pos = jnp.concatenate([start_ref[q_lo:q_lo + tile, :]] * (tile // HD), axis=1)
        visible = key_pos >= first_pos
        if causal:
            visible = visible & (key_pos <= lax.broadcasted_iota(jnp.int32, (tile, tile), 0) + q_lo)
        weights = jnp.where(visible, act, 0.0).astype(jnp.bfloat16)
        return jnp.dot(weights, value_tile, preferred_element_type=jnp.float32)

    def put(i, value, add):
        for part in range(tile // rows):
            at = i * (tile // rows) + part
            piece = value[part * rows:(part + 1) * rows]
            att[at] = att[at] + piece if add else piece

    for i in range(tiles):
        q = own_q[i * tile:(i + 1) * tile, :]
        acc = None
        for t in range(i + 1):
            span = slice(t * tile, (t + 1) * tile)
            term = attend(q, own_k[span, :], own_v[span, :], i * tile, t * tile, 0, t == i)
            acc = term if acc is None else acc + term
        put(i, acc, False)
    for offset in range(1, window + 1):
        @pl.when(my_ctx >= offset)
        def _():
            ctx_copy(0, own_k, prev_k, offset).wait_recv()
            ctx_copy(1, own_v, prev_v, offset).wait_recv()
            for i in range(tiles):
                q = own_q[i * tile:(i + 1) * tile, :]
                acc = None
                for t in range(i if offset == window else 0, tiles):
                    span = slice(t * tile, (t + 1) * tile)
                    term = attend(q, prev_k[offset - 1, span, :], prev_v[offset - 1, span, :],
                                  i * tile, t * tile, offset * row_count, False)
                    acc = term if acc is None else acc + term
                put(i, acc, True)

    source_other = sources[0]
    for j in range(1, per_owner):
        source_other = jnp.where(sides[j] == 1, sources[j], source_other)
    side_source = (sources[0], source_other)
    for c, (k, low, size) in enumerate(chunks):
        arrive(recv_u[c], 3 + c)
        for part in range(2):
            at = jnp.int32(0)
            for j in range(per_owner):
                at = jnp.where((ranks[j] == k) & (sides[j] == part), j, at)
            rows_f32 = att[at, low:low + size, :]
            mean_square = jnp.mean(rows_f32 * rows_f32, axis=-1, keepdims=True)
            normed = rows_f32 * lax.rsqrt(mean_square + 1e-06)
            update = recv_u[c][side_source[part]].astype(jnp.float32)
            gated[c][my_head, part * size:(part + 1) * size, :] = (normed * update).astype(jnp.bfloat16)
        for offset in range(1, heads):
            copy = pltpu.make_async_remote_copy(
                src_ref=gated[c].at[my_head], dst_ref=gated[c].at[my_head],
                send_sem=h_send.at[offset - 1], recv_sem=h_recv.at[c],
                device_id={"head": lax.rem(my_head + offset, heads)}, device_id_type=MESH)
            copy.start()
    for copy in w_copies:
        copy.wait_send()
    if heads > 1:
        all_cols = w_cols.at[pl.ds(0, heads - 1)]
        pltpu.make_async_copy(all_cols, all_cols, w_recv).wait()
    sent()
    for c, (k, low, size) in enumerate(chunks):
        if heads > 1:
            theirs = gated[c].at[pl.ds(0, heads - 1)]
            pltpu.make_async_copy(theirs, theirs, h_recv.at[c]).wait()
        acc = None
        for h in range(heads):
            term = jnp.dot(gated[c][h], w_cols[h], preferred_element_type=jnp.float32)
            acc = term if acc is None else acc + term
        acc = acc.astype(jnp.bfloat16)
        for side in range(2):
            mixed[2 * k + side, low:low + size, :] = acc[side * size:(side + 1) * size]
    for offset in range(1, heads):
        pltpu.make_async_remote_copy(
            src_ref=own_q, dst_ref=own_q, send_sem=h_send.at[offset - 1], recv_sem=h_recv.at[0],
            device_id={"head": my_head}, device_id_type=MESH).wait_send()
    for j in range(per_owner):
        out_ref[j * rows:(j + 1) * rows, :] = mixed[2 * ranks[j] + sides[j]]
    for offset in range(1, window + 1):
        @pl.when(my_ctx + offset < ctxs)
        def _():
            ctx_copy(0, own_k, prev_k, offset).wait_send()
            ctx_copy(1, own_v, prev_v, offset).wait_send()


def body(ingest, src_shard, src_slot, hist_len, w_out):
    groups, ctxs, heads = (lax.axis_size(a) for a in ("batch", "ctx", "head"))
    slot_total, rows, kinds, width = ingest.shape[2:]
    per_owner = src_shard.shape[2]
    capacity = per_owner // 2
    chunks = update_chunks(capacity, rows)
    half = groups // 2
    spans = max(half - 1, 1)
    window = ctxs // 2
    row_count = per_owner * rows
    bf16 = jnp.bfloat16
    dma = pltpu.SemaphoreType.DMA
    vmem = pl.BlockSpec(memory_space=pltpu.VMEM)
    mixed = pl.pallas_call(
        functools.partial(kernel, (groups, ctxs, heads, per_owner, rows)),
        out_shape=pltpu.VMEM((row_count, width), bf16),
        in_specs=[pl.BlockSpec(memory_space=pl.ANY)] * 5,
        out_specs=vmem,
        scratch_shapes=[
            pltpu.SMEM(src_shard.shape[1:], jnp.int32), pltpu.SMEM(src_slot.shape[1:], jnp.int32),
            pltpu.SMEM(hist_len.shape[1:], jnp.int32), pltpu.VMEM(w_out.shape, bf16), dma((4,)),
            [pltpu.VMEM((slot_total, size * kinds, width), bf16) for _, size in load_pieces(rows)],
            pltpu.VMEM((groups, 4 * capacity * rows, width), bf16),
            [pltpu.VMEM((groups, capacity, rows, width), bf16)] * 3,
            [pltpu.VMEM((groups, size, width), bf16) for _, _, size in chunks],
            pltpu.VMEM((spans, half, 4 * capacity * rows, width), bf16),
            pltpu.VMEM((row_count, width), bf16),
            pltpu.VMEM((row_count, width), bf16),
            pltpu.VMEM((row_count, width), bf16),
            pltpu.VMEM((window, row_count, width), bf16),
            pltpu.VMEM((window, row_count, width), bf16),
            pltpu.VMEM((row_count, width), jnp.int32),
            pltpu.VMEM((per_owner, rows, width), jnp.float32),
            [pltpu.VMEM((heads, 2 * size, width), bf16) for _, _, size in chunks],
            pltpu.VMEM((heads, width, width), bf16),
            pltpu.VMEM((per_owner, rows, width), bf16),
            dma((groups + spans * half,)), dma((3 + len(chunks) + 4 * spans * half,)),
            dma((2, window)), dma((2, window)),
            dma((max(heads - 1, 1),)), dma((len(chunks),)),
            dma((max(heads - 1, 1),)), dma,
            dma((2,)), pltpu.SemaphoreType.REGULAR((spans,)), pltpu.SemaphoreType.REGULAR((spans,)),
        ],
        compiler_params=pltpu.CompilerParams(
            collective_id=0, has_side_effects=True, vmem_limit_bytes=56 * 1024 * 1024),
    )(src_shard[0], src_slot[0], hist_len[0],
      ingest.reshape(slot_total, rows * kinds, width), w_out)
    return mixed[None]


def solution(mesh):
    in_specs = (
        P("ctx", "batch", None, None, None, "head"),
        P("ctx", None, None),
        P("ctx", None, None),
        P("batch", None),
        P("head", None),
    )
    out_specs = P("batch", "ctx", "head")
    return jax.shard_map(body, mesh=mesh, in_specs=in_specs, out_specs=out_specs, check_vma=False)
```

```python
import functools
import math

import jax
import jax.numpy as jnp
from jax import lax
from jax.experimental import pallas as pl
from jax.experimental.pallas import tpu as pltpu
from jax.sharding import PartitionSpec as P

HD = 128
MESH = pl.DeviceIdType.MESH
QUERY, KEY, VALUE, UPDATE = 0, 1, 2, 3
FIRST_KINDS = (KEY, VALUE, QUERY)
KINDS = (*FIRST_KINDS, UPDATE)
SPLIT = 2


def load_pieces(rows):
    return [(0, rows // 4), (rows // 4, rows - rows // 4)]


def unit_list(capacity, rows):
    units = [(KEY, 0, 0, low, size) for low, size in load_pieces(rows)]
    units += [(KEY, k, k, 0, rows) for k in range(1, capacity)]
    units += [(kind, k, k, 0, rows) for kind in FIRST_KINDS[1:] for k in range(capacity)]
    return units + [(UPDATE, c, *chunk) for c, chunk in enumerate(update_chunks(capacity, rows))]


def update_chunks(capacity, rows):
    size = rows // SPLIT
    return [(k, part * size, size) for k in range(capacity) for part in range(SPLIT)]


def kernel(sizes, shard_hbm, slot_hbm, hist_hbm, ingest_hbm, w_hbm, out_ref,
           shard_ref, slot_ref, hist_ref, w_ref, local_sems,
           ingest_refs,
           send_buf, recv_bufs, recv_u, relay_buf, own_k, own_v, own_q, prev_k, prev_v,
           start_ref, att, gated, w_cols, mixed,
           z_send, z_recv, c_send, c_recv, h_send, h_recv, w_send, w_recv,
           ingest_sems, from_low, from_high):
    groups, ctxs, heads, per_owner, rows = sizes
    capacity = per_owner // 2
    chunks = update_chunks(capacity, rows)
    window = ctxs // 2
    row_count = per_owner * rows
    my_group = lax.axis_index("batch")
    my_ctx = lax.axis_index("ctx")
    my_head = lax.axis_index("head")

    barrier = pltpu.get_barrier_semaphore()
    local_copies = [pltpu.make_async_copy(src, dst, local_sems.at[i]) for i, (src, dst) in enumerate((
        (shard_hbm, shard_ref), (slot_hbm, slot_ref), (hist_hbm, hist_ref), (w_hbm, w_ref)))]
    pieces = load_pieces(rows)
    kinds = ingest_hbm.shape[1] // rows
    ingest_copies = [pltpu.make_async_copy(
        ingest_hbm.at[:, pl.ds(low * kinds, size * kinds), :], ingest_refs[p], ingest_sems.at[p])
        for p, (low, size) in enumerate(pieces)]
    for copy in (*local_copies[:2], *ingest_copies, *local_copies[2:]):
        copy.start()
    for axis, me, count in (("ctx", my_ctx, ctxs), ("head", my_head, heads)):
        for offset in range(1, count):
            pl.semaphore_signal(barrier, inc=1, device_id={axis: lax.rem(me + offset, count)}, device_id_type=MESH)
    has_low, has_high = my_group > 0, my_group < groups - 1

    def tell(there, semaphore, to):
        @pl.when(there)
        def _():
            pl.semaphore_signal(semaphore, inc=1, device_id={"batch": to}, device_id_type=MESH)

    tell(has_low, barrier, my_group - 1)
    tell(has_high, barrier, my_group + 1)
    neighbours = jnp.where(has_low, 1, 0) + jnp.where(has_high, 1, 0)

    for copy in local_copies[:2]:
        copy.wait()
    slots = []
    for dst in range(groups):
        picked = [jnp.int32(0)] * capacity
        seen = jnp.int32(0)
        for j in range(per_owner):
            hit = shard_ref[dst, j] == my_group
            slot = slot_ref[dst, j]
            for k in range(capacity):
                picked[k] = jnp.where(hit & (seen == k), slot, picked[k])
            seen = seen + jnp.where(hit, 1, 0)
        slots.append(picked)

    sources = [shard_ref[my_group, j] for j in range(per_owner)]
    ranks, sides = [], []
    for j in range(per_owner):
        rank = jnp.int32(0)
        for i in range(j):
            rank = rank + jnp.where(sources[i] == sources[j], 1, 0)
        ranks.append(jnp.minimum(rank, capacity - 1))
        sides.append(jnp.where(sources[j] == sources[0], 0, 1))

    fine = rows // 4

    def split_kind(kind):
        row = lax.broadcasted_iota(jnp.int32, (fine, fine * kinds), 0)
        col = lax.broadcasted_iota(jnp.int32, (fine, fine * kinds), 1)
        pick = jnp.where(col == row * kinds + kind, 1.0, 0.0).astype(jnp.bfloat16)

        def one(dst, k, low):
            p = max(p for p, (first, _) in enumerate(pieces) if first <= low)
            at = (low - pieces[p][0]) * kinds
            block = ingest_refs[p][slots[dst][k], at:at + fine * kinds, :]
            return jnp.dot(pick, block, preferred_element_type=jnp.float32).astype(jnp.bfloat16)

        return one

    units = unit_list(capacity, rows)
    half = groups // 2
    low_side = my_group < half
    depth = jnp.where(low_side, half - 1 - my_group, my_group - half)

    def same(e):
        return jnp.where(low_side, half - 1 - e, half + e)

    def other(e):
        return jnp.where(low_side, half + e, half - 1 - e)

    def fill(kind, k, low, size):
        one = split_kind(kind)
        base = (KINDS.index(kind) * capacity + k) * rows
        for dst in range(groups):
            for at in range(low, low + size, fine):
                send_buf[dst, base + at:base + at + fine, :] = one(dst, k, at)

    def span(n):
        kind, _, k, low, size = units[n]
        return pl.ds((KINDS.index(kind) * capacity + k) * rows + low, size)

    def inbox(n, src):
        kind, c, k, low, size = units[n]
        return recv_u[c].at[src] if kind == UPDATE else recv_bufs[FIRST_KINDS.index(kind)].at[src, k, pl.ds(low, size)]

    def keep(kind):
        for n, unit in enumerate(units):
            if unit[0] == kind:
                inbox(n, my_group)[...] = send_buf[my_group, span(n), :]

    def z_copy(src, dst, out_id, in_id, to):
        return pltpu.make_async_remote_copy(
            src_ref=src, dst_ref=dst, send_sem=z_send.at[out_id], recv_sem=z_recv.at[in_id],
            device_id={"batch": to}, device_id_type=MESH)

    def here_id(n):
        kind, c = units[n][:2]
        return 3 + c if kind == UPDATE else FIRST_KINDS.index(kind)

    def relay_id(kind, far, e):
        return 3 + len(chunks) + (KINDS.index(kind) * (half - 1) + far - 1) * half + e

    def side_copy(n, e):
        return z_copy(send_buf.at[same(e), span(n)], inbox(n, my_group), e, here_id(n), same(e))

    def cross_copy(n, e):
        return z_copy(send_buf.at[other(e), span(n)], inbox(n, my_group), half + e, here_id(n), other(e))

    def relay_copy(n, far, e):
        return z_copy(send_buf.at[other(e), span(n)], relay_buf.at[far - 1, e, span(n)],
                      half + e, relay_id(units[n][0], far, e), same(0))

    def forward_copy(n, far, e):
        return z_copy(relay_buf.at[far - 1, e, span(n)], inbox(n, same(far)),
                      2 * half + (far - 1) * half + e, here_id(n), other(e))

    def side(n, middle):
        for here in range(half):
            if (here == 0) == middle and half > 1:
                @pl.when(depth == here)
                def _():
                    for e in range(half):
                        if e != here:
                            side_copy(n, e).start()

    def cross(n, e):
        @pl.when(depth == 0)
        def _():
            cross_copy(n, e).start()

    def to_middle(n, e):
        for here in range(1, half):
            @pl.when(depth == here)
            def _():
                relay_copy(n, here, e).start()

    relayed = set()

    def forward(n, e):
        kind = units[n][0]
        first = (kind, e) not in relayed
        relayed.add((kind, e))
        for far in range(1, half):
            @pl.when(depth == 0)
            def _():
                if first:
                    whole = relay_buf.at[far - 1, e, pl.ds(KINDS.index(kind) * capacity * rows, capacity * rows)]
                    z_copy(whole, whole, 0, relay_id(kind, far, e), my_group).wait_recv()
                forward_copy(n, far, e).start()

    def arrive(buf, in_id):
        others = buf.at[pl.ds(0, groups - 1)]
        z_copy(others, others, 0, in_id, my_group).wait_recv()

    def sent():
        whole = send_buf.at[0]
        for e in range(half):
            @pl.when(depth != e)
            def _():
                z_copy(whole, whole, e, 0, my_group).wait_send()
            z_copy(whole, whole, half + e, 0, my_group).wait_send()
        for flow in range(2 * half, half + half * half):
            @pl.when(depth == 0)
            def _():
                z_copy(whole, whole, flow, 0, my_group).wait_send()

    def collect(kind, own_ref):
        n = FIRST_KINDS.index(kind)
        arrive(recv_bufs[n], n)
        for j in range(per_owner):
            own_ref[j * rows:(j + 1) * rows, :] = recv_bufs[n][sources[j], ranks[j]]

    def hear(distance):
        for there, semaphore in ((my_group >= distance, from_low), (my_group + distance < groups, from_high)):
            @pl.when(there)
            def _():
                pl.semaphore_wait(semaphore.at[distance - 2], 1)

    def pass_on(distance):
        tell((my_group >= distance) & has_high, from_low.at[distance - 1], my_group + 1)
        tell((my_group + distance < groups) & has_low, from_high.at[distance - 1], my_group - 1)

    key_units, value_units, query_units = ([n for n, unit in enumerate(units) if unit[0] == want] for want in FIRST_KINDS)
    update_units = [n for n, unit in enumerate(units) if unit[0] == UPDATE]
    pairs = key_units + value_units
    far_first = list(range(half - 1, -1, -1))
    early = [(n, 0) for n in query_units]
    late_order = [(n, e) for group in (query_units, update_units) for e in far_first for n in group]

    ingest_copies[0].wait()
    fill(KEY, *units[0][2:])
    pl.semaphore_wait(barrier, neighbours + ctxs + heads - 2)
    for n in pairs:
        if n == 1:
            for copy in ingest_copies[1:]:
                copy.wait()
        if n > 0:
            fill(units[n][0], *units[n][2:])
        if n == 1:
            for distance in range(1, half):
                if distance > 1:
                    hear(distance)
                pass_on(distance)
        cross(n, 0)
        if n in key_units:
            to_middle(n, 0)
        side(n, True)
    for e in range(1, half):
        for n in pairs:
            to_middle(n, e)
    for n in value_units:
        to_middle(n, 0)
    for n in pairs:
        side(n, False)
    for n in query_units:
        fill(QUERY, *units[n][2:])
        cross(n, 0)
        side(n, True)
    for k in range(capacity):
        fill(UPDATE, k, 0, rows)
    for n in update_units:
        side(n, True)
    for n, e in late_order:
        to_middle(n, e)
    for n in query_units + update_units:
        side(n, False)
    for kind in KINDS:
        keep(kind)
    if half > 1:
        hear(half)
    for n in key_units:
        forward(n, 0)
    for e in range(1, half):
        for group in (key_units, value_units):
            for n in group:
                cross(n, e)
            for n in group:
                forward(n, e)
    for n in value_units:
        forward(n, 0)

    for copy in local_copies[2:]:
        copy.wait()
    w_copies = []
    for offset in range(1, heads):
        to = lax.rem(my_head + offset, heads)
        copy = pltpu.make_async_remote_copy(
            src_ref=w_ref.at[:, pl.ds(pl.multiple_of(to * HD, HD), HD)], dst_ref=w_cols.at[my_head],
            send_sem=w_send.at[offset - 1], recv_sem=w_recv,
            device_id={"head": to}, device_id_type=MESH)
        copy.start()
        w_copies.append(copy)
    w_cols[my_head] = w_ref[:, pl.ds(pl.multiple_of(my_head * HD, HD), HD)]

    ends, total = [], jnp.int32(0)
    for u in range(hist_ref.shape[0]):
        total = total + hist_ref[u]
        ends.append(total)
    base = my_ctx * row_count
    position = base + lax.broadcasted_iota(jnp.int32, (row_count, HD), 0)
    first = jnp.zeros((row_count, HD), jnp.int32)
    for end in ends:
        first = jnp.where(position >= end, end, first)
    start_ref[...] = first - base

    def ctx_copy(n, own_ref, prev_ref, offset):
        return pltpu.make_async_remote_copy(
            src_ref=own_ref, dst_ref=prev_ref.at[offset - 1],
            send_sem=c_send.at[n, offset - 1], recv_sem=c_recv.at[n, offset - 1],
            device_id={"ctx": lax.rem(my_ctx + offset, ctxs)}, device_id_type=MESH)

    def push(n, own_ref, prev_ref):
        for offset in range(1, window + 1):
            @pl.when(my_ctx + offset < ctxs)
            def _():
                ctx_copy(n, own_ref, prev_ref, offset).start()

    collect(KEY, own_k)
    push(0, own_k, prev_k)
    for n, e in late_order:
        if n in query_units and e > 0:
            cross(n, e)
            forward(n, e)
    collect(VALUE, own_v)
    push(1, own_v, prev_v)
    for n, e in late_order:
        if n in query_units and e > 0:
            continue
        if (n, e) not in early:
            cross(n, e)
        forward(n, e)
    collect(QUERY, own_q)

    tile = 2 * rows if per_owner % 2 == 0 else rows
    tiles = row_count // tile
    half_scale = 0.5 / math.sqrt(HD)

    def attend(q, key_tile, value_tile, q_lo, k_lo, shift, causal):
        scores = lax.dot_general(q, key_tile, (((1,), (1,)), ((), ())), preferred_element_type=jnp.float32)
        half = scores * half_scale
        act = half + half * jnp.tanh(half)
        key_pos = lax.broadcasted_iota(jnp.int32, (tile, tile), 1) + (k_lo - shift)
        first_pos = jnp.concatenate([start_ref[q_lo:q_lo + tile, :]] * (tile // HD), axis=1)
        visible = key_pos >= first_pos
        if causal:
            visible = visible & (key_pos <= lax.broadcasted_iota(jnp.int32, (tile, tile), 0) + q_lo)
        weights = jnp.where(visible, act, 0.0).astype(jnp.bfloat16)
        return jnp.dot(weights, value_tile, preferred_element_type=jnp.float32)

    def put(i, value, add):
        for part in range(tile // rows):
            at = i * (tile // rows) + part
            piece = value[part * rows:(part + 1) * rows]
            att[at] = att[at] + piece if add else piece

    for i in range(tiles):
        q = own_q[i * tile:(i + 1) * tile, :]
        acc = None
        for t in range(i + 1):
            span = slice(t * tile, (t + 1) * tile)
            term = attend(q, own_k[span, :], own_v[span, :], i * tile, t * tile, 0, t == i)
            acc = term if acc is None else acc + term
        put(i, acc, False)
    for offset in range(1, window + 1):
        @pl.when(my_ctx >= offset)
        def _():
            ctx_copy(0, own_k, prev_k, offset).wait_recv()
            ctx_copy(1, own_v, prev_v, offset).wait_recv()
            for i in range(tiles):
                q = own_q[i * tile:(i + 1) * tile, :]
                acc = None
                for t in range(i if offset == window else 0, tiles):
                    span = slice(t * tile, (t + 1) * tile)
                    term = attend(q, prev_k[offset - 1, span, :], prev_v[offset - 1, span, :],
                                  i * tile, t * tile, offset * row_count, False)
                    acc = term if acc is None else acc + term
                put(i, acc, True)

    source_other = sources[0]
    for j in range(1, per_owner):
        source_other = jnp.where(sides[j] == 1, sources[j], source_other)
    side_source = (sources[0], source_other)
    for c, (k, low, size) in enumerate(chunks):
        arrive(recv_u[c], 3 + c)
        for part in range(2):
            at = jnp.int32(0)
            for j in range(per_owner):
                at = jnp.where((ranks[j] == k) & (sides[j] == part), j, at)
            rows_f32 = att[at, low:low + size, :]
            mean_square = jnp.mean(rows_f32 * rows_f32, axis=-1, keepdims=True)
            normed = rows_f32 * lax.rsqrt(mean_square + 1e-06)
            update = recv_u[c][side_source[part]].astype(jnp.float32)
            gated[c][my_head, part * size:(part + 1) * size, :] = (normed * update).astype(jnp.bfloat16)
        for offset in range(1, heads):
            copy = pltpu.make_async_remote_copy(
                src_ref=gated[c].at[my_head], dst_ref=gated[c].at[my_head],
                send_sem=h_send.at[offset - 1], recv_sem=h_recv.at[c],
                device_id={"head": lax.rem(my_head + offset, heads)}, device_id_type=MESH)
            copy.start()
    for copy in w_copies:
        copy.wait_send()
    if heads > 1:
        all_cols = w_cols.at[pl.ds(0, heads - 1)]
        pltpu.make_async_copy(all_cols, all_cols, w_recv).wait()
    sent()
    for c, (k, low, size) in enumerate(chunks):
        if heads > 1:
            theirs = gated[c].at[pl.ds(0, heads - 1)]
            pltpu.make_async_copy(theirs, theirs, h_recv.at[c]).wait()
        acc = None
        for h in range(heads):
            term = jnp.dot(gated[c][h], w_cols[h], preferred_element_type=jnp.float32)
            acc = term if acc is None else acc + term
        acc = acc.astype(jnp.bfloat16)
        for side in range(2):
            mixed[2 * k + side, low:low + size, :] = acc[side * size:(side + 1) * size]
    for offset in range(1, heads):
        pltpu.make_async_remote_copy(
            src_ref=own_q, dst_ref=own_q, send_sem=h_send.at[offset - 1], recv_sem=h_recv.at[0],
            device_id={"head": my_head}, device_id_type=MESH).wait_send()
    for j in range(per_owner):
        out_ref[j * rows:(j + 1) * rows, :] = mixed[2 * ranks[j] + sides[j]]
    for offset in range(1, window + 1):
        @pl.when(my_ctx + offset < ctxs)
        def _():
            ctx_copy(0, own_k, prev_k, offset).wait_send()
            ctx_copy(1, own_v, prev_v, offset).wait_send()


def body(ingest, src_shard, src_slot, hist_len, w_out):
    groups, ctxs, heads = (lax.axis_size(a) for a in ("batch", "ctx", "head"))
    slot_total, rows, kinds, width = ingest.shape[2:]
    per_owner = src_shard.shape[2]
    capacity = per_owner // 2
    chunks = update_chunks(capacity, rows)
    half = groups // 2
    spans = max(half - 1, 1)
    window = ctxs // 2
    row_count = per_owner * rows
    bf16 = jnp.bfloat16
    dma = pltpu.SemaphoreType.DMA
    vmem = pl.BlockSpec(memory_space=pltpu.VMEM)
    mixed = pl.pallas_call(
        functools.partial(kernel, (groups, ctxs, heads, per_owner, rows)),
        out_shape=pltpu.VMEM((row_count, width), bf16),
        in_specs=[pl.BlockSpec(memory_space=pl.ANY)] * 5,
        out_specs=vmem,
        scratch_shapes=[
            pltpu.SMEM(src_shard.shape[1:], jnp.int32), pltpu.SMEM(src_slot.shape[1:], jnp.int32),
            pltpu.SMEM(hist_len.shape[1:], jnp.int32), pltpu.VMEM(w_out.shape, bf16), dma((4,)),
            [pltpu.VMEM((slot_total, size * kinds, width), bf16) for _, size in load_pieces(rows)],
            pltpu.VMEM((groups, 4 * capacity * rows, width), bf16),
            [pltpu.VMEM((groups, capacity, rows, width), bf16)] * 3,
            [pltpu.VMEM((groups, size, width), bf16) for _, _, size in chunks],
            pltpu.VMEM((spans, half, 4 * capacity * rows, width), bf16),
            pltpu.VMEM((row_count, width), bf16),
            pltpu.VMEM((row_count, width), bf16),
            pltpu.VMEM((row_count, width), bf16),
            pltpu.VMEM((window, row_count, width), bf16),
            pltpu.VMEM((window, row_count, width), bf16),
            pltpu.VMEM((row_count, width), jnp.int32),
            pltpu.VMEM((per_owner, rows, width), jnp.float32),
            [pltpu.VMEM((heads, 2 * size, width), bf16) for _, _, size in chunks],
            pltpu.VMEM((heads, width, width), bf16),
            pltpu.VMEM((per_owner, rows, width), bf16),
            dma((groups + spans * half,)), dma((3 + len(chunks) + 4 * spans * half,)),
            dma((2, window)), dma((2, window)),
            dma((max(heads - 1, 1),)), dma((len(chunks),)),
            dma((max(heads - 1, 1),)), dma,
            dma((2,)), pltpu.SemaphoreType.REGULAR((spans,)), pltpu.SemaphoreType.REGULAR((spans,)),
        ],
        compiler_params=pltpu.CompilerParams(
            collective_id=0, has_side_effects=True, vmem_limit_bytes=56 * 1024 * 1024),
    )(src_shard[0], src_slot[0], hist_len[0],
      ingest.reshape(slot_total, rows * kinds, width), w_out)
    return mixed[None]


def solution(mesh):
    in_specs = (
        P("ctx", "batch", None, None, None, "head"),
        P("ctx", None, None),
        P("ctx", None, None),
        P("batch", None),
        P("head", None),
    )
    out_specs = P("batch", "ctx", "head")
    return jax.shard_map(body, mesh=mesh, in_specs=in_specs, out_specs=out_specs, check_vma=False)
```

```python
import functools
import math

import jax
import jax.numpy as jnp
from jax import lax
from jax.experimental import pallas as pl
from jax.experimental.pallas import tpu as pltpu
from jax.sharding import PartitionSpec as P

HD = 128
MESH = pl.DeviceIdType.MESH
QUERY, KEY, VALUE, UPDATE = 0, 1, 2, 3
FIRST_KINDS = (KEY, VALUE, QUERY)
KINDS = (*FIRST_KINDS, UPDATE)
SPLIT = 2


def load_pieces(rows):
    return [(0, rows // 4), (rows // 4, rows - rows // 4)]


def unit_list(capacity, rows):
    units = [(KEY, 0, 0, low, size) for low, size in load_pieces(rows)]
    units += [(KEY, k, k, 0, rows) for k in range(1, capacity)]
    units += [(kind, k, k, 0, rows) for kind in FIRST_KINDS[1:] for k in range(capacity)]
    return units + [(UPDATE, c, *chunk) for c, chunk in enumerate(update_chunks(capacity, rows))]


def update_chunks(capacity, rows):
    size = rows // SPLIT
    return [(k, part * size, size) for k in range(capacity) for part in range(SPLIT)]


def kernel(sizes, shard_hbm, slot_hbm, hist_hbm, ingest_hbm, w_hbm, out_ref,
           shard_ref, slot_ref, hist_ref, w_ref, local_sems,
           ingest_refs,
           send_buf, recv_bufs, recv_u, relay_buf, own_k, own_v, own_q, prev_k, prev_v,
           start_ref, att, gated, w_cols, mixed,
           z_send, z_recv, c_send, c_recv, h_send, h_recv, w_send, w_recv,
           ingest_sems, from_low, from_high):
    groups, ctxs, heads, per_owner, rows = sizes
    capacity = per_owner // 2
    chunks = update_chunks(capacity, rows)
    window = ctxs // 2
    row_count = per_owner * rows
    my_group = lax.axis_index("batch")
    my_ctx = lax.axis_index("ctx")
    my_head = lax.axis_index("head")

    barrier = pltpu.get_barrier_semaphore()
    local_copies = [pltpu.make_async_copy(src, dst, local_sems.at[i]) for i, (src, dst) in enumerate((
        (shard_hbm, shard_ref), (slot_hbm, slot_ref), (hist_hbm, hist_ref), (w_hbm, w_ref)))]
    pieces = load_pieces(rows)
    kinds = ingest_hbm.shape[1] // rows
    ingest_copies = [pltpu.make_async_copy(
        ingest_hbm.at[:, pl.ds(low * kinds, size * kinds), :], ingest_refs[p], ingest_sems.at[p])
        for p, (low, size) in enumerate(pieces)]
    for copy in (*local_copies[:2], *ingest_copies, *local_copies[2:]):
        copy.start()
    for axis, me, count in (("ctx", my_ctx, ctxs), ("head", my_head, heads)):
        for offset in range(1, count):
            pl.semaphore_signal(barrier, inc=1, device_id={axis: lax.rem(me + offset, count)}, device_id_type=MESH)
    has_low, has_high = my_group > 0, my_group < groups - 1

    def tell(there, semaphore, to):
        @pl.when(there)
        def _():
            pl.semaphore_signal(semaphore, inc=1, device_id={"batch": to}, device_id_type=MESH)

    tell(has_low, barrier, my_group - 1)
    tell(has_high, barrier, my_group + 1)
    neighbours = jnp.where(has_low, 1, 0) + jnp.where(has_high, 1, 0)

    for copy in local_copies[:2]:
        copy.wait()
    slots = []
    for dst in range(groups):
        picked = [jnp.int32(0)] * capacity
        seen = jnp.int32(0)
        for j in range(per_owner):
            hit = shard_ref[dst, j] == my_group
            slot = slot_ref[dst, j]
            for k in range(capacity):
                picked[k] = jnp.where(hit & (seen == k), slot, picked[k])
            seen = seen + jnp.where(hit, 1, 0)
        slots.append(picked)

    sources = [shard_ref[my_group, j] for j in range(per_owner)]
    ranks, sides = [], []
    for j in range(per_owner):
        rank = jnp.int32(0)
        for i in range(j):
            rank = rank + jnp.where(sources[i] == sources[j], 1, 0)
        ranks.append(jnp.minimum(rank, capacity - 1))
        sides.append(jnp.where(sources[j] == sources[0], 0, 1))

    fine = rows // 4

    def split_kind(kind):
        row = lax.broadcasted_iota(jnp.int32, (fine, fine * kinds), 0)
        col = lax.broadcasted_iota(jnp.int32, (fine, fine * kinds), 1)
        pick = jnp.where(col == row * kinds + kind, 1.0, 0.0).astype(jnp.bfloat16)

        def one(dst, k, low):
            p = max(p for p, (first, _) in enumerate(pieces) if first <= low)
            at = (low - pieces[p][0]) * kinds
            block = ingest_refs[p][slots[dst][k], at:at + fine * kinds, :]
            return jnp.dot(pick, block, preferred_element_type=jnp.float32).astype(jnp.bfloat16)

        return one

    units = unit_list(capacity, rows)
    half = groups // 2
    low_side = my_group < half
    depth = jnp.where(low_side, half - 1 - my_group, my_group - half)

    def same(e):
        return jnp.where(low_side, half - 1 - e, half + e)

    def other(e):
        return jnp.where(low_side, half + e, half - 1 - e)

    def fill(kind, k, low, size):
        one = split_kind(kind)
        base = (KINDS.index(kind) * capacity + k) * rows
        for dst in range(groups):
            for at in range(low, low + size, fine):
                send_buf[dst, base + at:base + at + fine, :] = one(dst, k, at)

    def span(n):
        kind, _, k, low, size = units[n]
        return pl.ds((KINDS.index(kind) * capacity + k) * rows + low, size)

    def inbox(n, src):
        kind, c, k, low, size = units[n]
        return recv_u[c].at[src] if kind == UPDATE else recv_bufs[FIRST_KINDS.index(kind)].at[src, k, pl.ds(low, size)]

    def keep(kind):
        for n, unit in enumerate(units):
            if unit[0] == kind:
                inbox(n, my_group)[...] = send_buf[my_group, span(n), :]

    def z_copy(src, dst, out_id, in_id, to):
        return pltpu.make_async_remote_copy(
            src_ref=src, dst_ref=dst, send_sem=z_send.at[out_id], recv_sem=z_recv.at[in_id],
            device_id={"batch": to}, device_id_type=MESH)

    def here_id(n):
        kind, c = units[n][:2]
        return 3 + c if kind == UPDATE else FIRST_KINDS.index(kind)

    def relay_id(kind, far, e):
        return 3 + len(chunks) + (KINDS.index(kind) * (half - 1) + far - 1) * half + e

    def side_copy(n, e):
        return z_copy(send_buf.at[same(e), span(n)], inbox(n, my_group), e, here_id(n), same(e))

    def cross_copy(n, e):
        return z_copy(send_buf.at[other(e), span(n)], inbox(n, my_group), half + e, here_id(n), other(e))

    def relay_copy(n, far, e):
        return z_copy(send_buf.at[other(e), span(n)], relay_buf.at[far - 1, e, span(n)],
                      half + e, relay_id(units[n][0], far, e), same(0))

    def forward_copy(n, far, e):
        return z_copy(relay_buf.at[far - 1, e, span(n)], inbox(n, same(far)),
                      2 * half + (far - 1) * half + e, here_id(n), other(e))

    def side(n, middle):
        for here in range(half):
            if (here == 0) == middle and half > 1:
                @pl.when(depth == here)
                def _():
                    for e in range(half):
                        if e != here:
                            side_copy(n, e).start()

    def cross(n, e):
        @pl.when(depth == 0)
        def _():
            cross_copy(n, e).start()

    def to_middle(n, e):
        for here in range(1, half):
            @pl.when(depth == here)
            def _():
                relay_copy(n, here, e).start()

    relayed = set()

    def forward(n, e):
        kind = units[n][0]
        first = (kind, e) not in relayed
        relayed.add((kind, e))
        for far in range(1, half):
            @pl.when(depth == 0)
            def _():
                if first:
                    whole = relay_buf.at[far - 1, e, pl.ds(KINDS.index(kind) * capacity * rows, capacity * rows)]
                    z_copy(whole, whole, 0, relay_id(kind, far, e), my_group).wait_recv()
                forward_copy(n, far, e).start()

    def arrive(buf, in_id):
        others = buf.at[pl.ds(0, groups - 1)]
        z_copy(others, others, 0, in_id, my_group).wait_recv()

    def sent():
        whole = send_buf.at[0]
        for e in range(half):
            @pl.when(depth != e)
            def _():
                z_copy(whole, whole, e, 0, my_group).wait_send()
            z_copy(whole, whole, half + e, 0, my_group).wait_send()
        for flow in range(2 * half, half + half * half):
            @pl.when(depth == 0)
            def _():
                z_copy(whole, whole, flow, 0, my_group).wait_send()

    def collect(kind, own_ref):
        n = FIRST_KINDS.index(kind)
        arrive(recv_bufs[n], n)
        for j in range(per_owner):
            own_ref[j * rows:(j + 1) * rows, :] = recv_bufs[n][sources[j], ranks[j]]

    def hear(distance):
        for there, semaphore in ((my_group >= distance, from_low), (my_group + distance < groups, from_high)):
            @pl.when(there)
            def _():
                pl.semaphore_wait(semaphore.at[distance - 2], 1)

    def pass_on(distance):
        tell((my_group >= distance) & has_high, from_low.at[distance - 1], my_group + 1)
        tell((my_group + distance < groups) & has_low, from_high.at[distance - 1], my_group - 1)

    key_units, value_units, query_units = ([n for n, unit in enumerate(units) if unit[0] == want] for want in FIRST_KINDS)
    update_units = [n for n, unit in enumerate(units) if unit[0] == UPDATE]
    pairs = key_units + value_units
    far_first = list(range(half - 1, -1, -1))
    early = [(n, 0) for n in query_units]
    late_order = [(n, e) for group in (query_units, update_units) for e in far_first for n in group]

    ingest_copies[0].wait()
    fill(KEY, *units[0][2:])
    pl.semaphore_wait(barrier, neighbours + ctxs + heads - 2)
    for n in pairs:
        if n == 1:
            for copy in ingest_copies[1:]:
                copy.wait()
        if n > 0:
            fill(units[n][0], *units[n][2:])
        if n == 1:
            for distance in range(1, half):
                if distance > 1:
                    hear(distance)
                pass_on(distance)
        cross(n, 0)
        if n in key_units:
            to_middle(n, 0)
        side(n, True)
    for e in range(1, half):
        for n in pairs:
            to_middle(n, e)
    for n in value_units:
        to_middle(n, 0)
    for n in pairs:
        side(n, False)
    for n in query_units:
        fill(QUERY, *units[n][2:])
        cross(n, 0)
        side(n, True)
    for k in range(capacity):
        fill(UPDATE, k, 0, rows)
    for n in update_units:
        side(n, True)
    for n, e in late_order:
        to_middle(n, e)
    for n in query_units + update_units:
        side(n, False)
    for kind in KINDS:
        keep(kind)
    if half > 1:
        hear(half)
    for n in key_units:
        forward(n, 0)
    for e in range(1, half):
        for group in (key_units, value_units):
            for n in group:
                cross(n, e)
            for n in group:
                forward(n, e)
    for n in value_units:
        forward(n, 0)

    for copy in local_copies[2:]:
        copy.wait()
    w_copies = []
    for offset in range(1, heads):
        to = lax.rem(my_head + offset, heads)
        copy = pltpu.make_async_remote_copy(
            src_ref=w_ref.at[:, pl.ds(pl.multiple_of(to * HD, HD), HD)], dst_ref=w_cols.at[my_head],
            send_sem=w_send.at[offset - 1], recv_sem=w_recv,
            device_id={"head": to}, device_id_type=MESH)
        copy.start()
        w_copies.append(copy)
    w_cols[my_head] = w_ref[:, pl.ds(pl.multiple_of(my_head * HD, HD), HD)]

    ends, total = [], jnp.int32(0)
    for u in range(hist_ref.shape[0]):
        total = total + hist_ref[u]
        ends.append(total)
    base = my_ctx * row_count
    position = base + lax.broadcasted_iota(jnp.int32, (row_count, HD), 0)
    first = jnp.zeros((row_count, HD), jnp.int32)
    for end in ends:
        first = jnp.where(position >= end, end, first)
    start_ref[...] = first - base

    def ctx_copy(n, own_ref, prev_ref, offset):
        return pltpu.make_async_remote_copy(
            src_ref=own_ref, dst_ref=prev_ref.at[offset - 1],
            send_sem=c_send.at[n, offset - 1], recv_sem=c_recv.at[n, offset - 1],
            device_id={"ctx": lax.rem(my_ctx + offset, ctxs)}, device_id_type=MESH)

    def push(n, own_ref, prev_ref):
        for offset in range(1, window + 1):
            @pl.when(my_ctx + offset < ctxs)
            def _():
                ctx_copy(n, own_ref, prev_ref, offset).start()

    collect(KEY, own_k)
    push(0, own_k, prev_k)
    for n, e in late_order:
        if n in query_units and e > 0:
            cross(n, e)
            forward(n, e)
    collect(VALUE, own_v)
    push(1, own_v, prev_v)
    for n, e in late_order:
        if n in query_units and e > 0:
            continue
        if (n, e) not in early:
            cross(n, e)
        forward(n, e)
    collect(QUERY, own_q)

    tile = 2 * rows if per_owner % 2 == 0 else rows
    tiles = row_count // tile
    half_scale = 0.5 / math.sqrt(HD)

    def attend(q, key_tile, value_tile, q_lo, k_lo, shift, causal):
        scores = lax.dot_general(q, key_tile, (((1,), (1,)), ((), ())), preferred_element_type=jnp.float32)
        half = scores * half_scale
        act = half + half * jnp.tanh(half)
        key_pos = lax.broadcasted_iota(jnp.int32, (tile, tile), 1) + (k_lo - shift)
        first_pos = jnp.concatenate([start_ref[q_lo:q_lo + tile, :]] * (tile // HD), axis=1)
        visible = key_pos >= first_pos
        if causal:
            visible = visible & (key_pos <= lax.broadcasted_iota(jnp.int32, (tile, tile), 0) + q_lo)
        weights = jnp.where(visible, act, 0.0).astype(jnp.bfloat16)
        return jnp.dot(weights, value_tile, preferred_element_type=jnp.float32)

    def put(i, value, add):
        for part in range(tile // rows):
            at = i * (tile // rows) + part
            piece = value[part * rows:(part + 1) * rows]
            att[at] = att[at] + piece if add else piece

    for i in range(tiles):
        q = own_q[i * tile:(i + 1) * tile, :]
        acc = None
        for t in range(i + 1):
            span = slice(t * tile, (t + 1) * tile)
            term = attend(q, own_k[span, :], own_v[span, :], i * tile, t * tile, 0, t == i)
            acc = term if acc is None else acc + term
        put(i, acc, False)
    for offset in range(1, window + 1):
        @pl.when(my_ctx >= offset)
        def _():
            ctx_copy(0, own_k, prev_k, offset).wait_recv()
            ctx_copy(1, own_v, prev_v, offset).wait_recv()
            for i in range(tiles):
                q = own_q[i * tile:(i + 1) * tile, :]
                acc = None
                for t in range(i if offset == window else 0, tiles):
                    span = slice(t * tile, (t + 1) * tile)
                    term = attend(q, prev_k[offset - 1, span, :], prev_v[offset - 1, span, :],
                                  i * tile, t * tile, offset * row_count, False)
                    acc = term if acc is None else acc + term
                put(i, acc, True)

    for j in range(per_owner):
        rows_f32 = att[j]
        mean_square = jnp.mean(rows_f32 * rows_f32, axis=-1, keepdims=True)
        att[j] = rows_f32 * lax.rsqrt(mean_square + 1e-06)

    source_other = sources[0]
    for j in range(1, per_owner):
        source_other = jnp.where(sides[j] == 1, sources[j], source_other)
    side_source = (sources[0], source_other)
    for c, (k, low, size) in enumerate(chunks):
        arrive(recv_u[c], 3 + c)
        for part in range(2):
            at = jnp.int32(0)
            for j in range(per_owner):
                at = jnp.where((ranks[j] == k) & (sides[j] == part), j, at)
            normed = att[at, low:low + size, :]
            update = recv_u[c][side_source[part]].astype(jnp.float32)
            gated[c][my_head, part * size:(part + 1) * size, :] = (normed * update).astype(jnp.bfloat16)
        for offset in range(1, heads):
            copy = pltpu.make_async_remote_copy(
                src_ref=gated[c].at[my_head], dst_ref=gated[c].at[my_head],
                send_sem=h_send.at[offset - 1], recv_sem=h_recv.at[c],
                device_id={"head": lax.rem(my_head + offset, heads)}, device_id_type=MESH)
            copy.start()
    for copy in w_copies:
        copy.wait_send()
    if heads > 1:
        all_cols = w_cols.at[pl.ds(0, heads - 1)]
        pltpu.make_async_copy(all_cols, all_cols, w_recv).wait()
    sent()
    for c, (k, low, size) in enumerate(chunks):
        if heads > 1:
            theirs = gated[c].at[pl.ds(0, heads - 1)]
            pltpu.make_async_copy(theirs, theirs, h_recv.at[c]).wait()
        acc = None
        for h in range(heads):
            term = jnp.dot(gated[c][h], w_cols[h], preferred_element_type=jnp.float32)
            acc = term if acc is None else acc + term
        acc = acc.astype(jnp.bfloat16)
        for side in range(2):
            mixed[2 * k + side, low:low + size, :] = acc[side * size:(side + 1) * size]
    for offset in range(1, heads):
        pltpu.make_async_remote_copy(
            src_ref=own_q, dst_ref=own_q, send_sem=h_send.at[offset - 1], recv_sem=h_recv.at[0],
            device_id={"head": my_head}, device_id_type=MESH).wait_send()
    for j in range(per_owner):
        out_ref[j * rows:(j + 1) * rows, :] = mixed[2 * ranks[j] + sides[j]]
    for offset in range(1, window + 1):
        @pl.when(my_ctx + offset < ctxs)
        def _():
            ctx_copy(0, own_k, prev_k, offset).wait_send()
            ctx_copy(1, own_v, prev_v, offset).wait_send()


def body(ingest, src_shard, src_slot, hist_len, w_out):
    groups, ctxs, heads = (lax.axis_size(a) for a in ("batch", "ctx", "head"))
    slot_total, rows, kinds, width = ingest.shape[2:]
    per_owner = src_shard.shape[2]
    capacity = per_owner // 2
    chunks = update_chunks(capacity, rows)
    half = groups // 2
    spans = max(half - 1, 1)
    window = ctxs // 2
    row_count = per_owner * rows
    bf16 = jnp.bfloat16
    dma = pltpu.SemaphoreType.DMA
    vmem = pl.BlockSpec(memory_space=pltpu.VMEM)
    mixed = pl.pallas_call(
        functools.partial(kernel, (groups, ctxs, heads, per_owner, rows)),
        out_shape=pltpu.VMEM((row_count, width), bf16),
        in_specs=[pl.BlockSpec(memory_space=pl.ANY)] * 5,
        out_specs=vmem,
        scratch_shapes=[
            pltpu.SMEM(src_shard.shape[1:], jnp.int32), pltpu.SMEM(src_slot.shape[1:], jnp.int32),
            pltpu.SMEM(hist_len.shape[1:], jnp.int32), pltpu.VMEM(w_out.shape, bf16), dma((4,)),
            [pltpu.VMEM((slot_total, size * kinds, width), bf16) for _, size in load_pieces(rows)],
            pltpu.VMEM((groups, 4 * capacity * rows, width), bf16),
            [pltpu.VMEM((groups, capacity, rows, width), bf16)] * 3,
            [pltpu.VMEM((groups, size, width), bf16) for _, _, size in chunks],
            pltpu.VMEM((spans, half, 4 * capacity * rows, width), bf16),
            pltpu.VMEM((row_count, width), bf16),
            pltpu.VMEM((row_count, width), bf16),
            pltpu.VMEM((row_count, width), bf16),
            pltpu.VMEM((window, row_count, width), bf16),
            pltpu.VMEM((window, row_count, width), bf16),
            pltpu.VMEM((row_count, width), jnp.int32),
            pltpu.VMEM((per_owner, rows, width), jnp.float32),
            [pltpu.VMEM((heads, 2 * size, width), bf16) for _, _, size in chunks],
            pltpu.VMEM((heads, width, width), bf16),
            pltpu.VMEM((per_owner, rows, width), bf16),
            dma((groups + spans * half,)), dma((3 + len(chunks) + 4 * spans * half,)),
            dma((2, window)), dma((2, window)),
            dma((max(heads - 1, 1),)), dma((len(chunks),)),
            dma((max(heads - 1, 1),)), dma,
            dma((2,)), pltpu.SemaphoreType.REGULAR((spans,)), pltpu.SemaphoreType.REGULAR((spans,)),
        ],
        compiler_params=pltpu.CompilerParams(
            collective_id=0, has_side_effects=True, vmem_limit_bytes=56 * 1024 * 1024),
    )(src_shard[0], src_slot[0], hist_len[0],
      ingest.reshape(slot_total, rows * kinds, width), w_out)
    return mixed[None]


def solution(mesh):
    in_specs = (
        P("ctx", "batch", None, None, None, "head"),
        P("ctx", None, None),
        P("ctx", None, None),
        P("batch", None),
        P("head", None),
    )
    out_specs = P("batch", "ctx", "head")
    return jax.shard_map(body, mesh=mesh, in_specs=in_specs, out_specs=out_specs, check_vma=False)
```

```python
import functools
import math

import jax
import jax.numpy as jnp
from jax import lax
from jax.experimental import pallas as pl
from jax.experimental.pallas import tpu as pltpu
from jax.sharding import PartitionSpec as P

HD = 128
MESH = pl.DeviceIdType.MESH
QUERY, KEY, VALUE, UPDATE = 0, 1, 2, 3
FIRST_KINDS = (KEY, VALUE, QUERY)
KINDS = (*FIRST_KINDS, UPDATE)
SPLIT = 4
TOGETHER = 2


def load_pieces(rows):
    return [(0, rows // 4), (rows // 4, rows - rows // 4)]


def unit_list(capacity, rows):
    units = [(KEY, 0, 0, low, size) for low, size in load_pieces(rows)]
    units += [(KEY, k, k, 0, rows) for k in range(1, capacity)]
    units += [(kind, k, k, 0, rows) for kind in FIRST_KINDS[1:] for k in range(capacity)]
    return units + [(UPDATE, c, *chunk) for c, chunk in enumerate(update_chunks(capacity, rows))]


def update_chunks(capacity, rows):
    size = rows // SPLIT
    return [(k, part * size, size) for k in range(capacity) for part in range(SPLIT)]


def kernel(sizes, shard_hbm, slot_hbm, hist_hbm, ingest_hbm, w_hbm, out_ref,
           shard_ref, slot_ref, hist_ref, w_ref, local_sems,
           ingest_refs,
           send_buf, recv_bufs, recv_u, relay_buf, own_k, own_v, own_q, prev_k, prev_v,
           start_ref, att, gated, w_cols, mixed,
           z_send, z_recv, c_send, c_recv, h_send, h_recv, w_send, w_recv,
           ingest_sems, from_low, from_high):
    groups, ctxs, heads, per_owner, rows = sizes
    capacity = per_owner // 2
    chunks = update_chunks(capacity, rows)
    window = ctxs // 2
    row_count = per_owner * rows
    my_group = lax.axis_index("batch")
    my_ctx = lax.axis_index("ctx")
    my_head = lax.axis_index("head")

    barrier = pltpu.get_barrier_semaphore()
    local_copies = [pltpu.make_async_copy(src, dst, local_sems.at[i]) for i, (src, dst) in enumerate((
        (shard_hbm, shard_ref), (slot_hbm, slot_ref), (hist_hbm, hist_ref), (w_hbm, w_ref)))]
    pieces = load_pieces(rows)
    kinds = ingest_hbm.shape[1] // rows
    ingest_copies = [pltpu.make_async_copy(
        ingest_hbm.at[:, pl.ds(low * kinds, size * kinds), :], ingest_refs[p], ingest_sems.at[p])
        for p, (low, size) in enumerate(pieces)]
    for copy in (*local_copies[:2], *ingest_copies, *local_copies[2:]):
        copy.start()
    for axis, me, count in (("ctx", my_ctx, ctxs), ("head", my_head, heads)):
        for offset in range(1, count):
            pl.semaphore_signal(barrier, inc=1, device_id={axis: lax.rem(me + offset, count)}, device_id_type=MESH)
    has_low, has_high = my_group > 0, my_group < groups - 1

    def tell(there, semaphore, to):
        @pl.when(there)
        def _():
            pl.semaphore_signal(semaphore, inc=1, device_id={"batch": to}, device_id_type=MESH)

    tell(has_low, barrier, my_group - 1)
    tell(has_high, barrier, my_group + 1)
    neighbours = jnp.where(has_low, 1, 0) + jnp.where(has_high, 1, 0)

    for copy in local_copies[:2]:
        copy.wait()
    slots = []
    for dst in range(groups):
        picked = [jnp.int32(0)] * capacity
        seen = jnp.int32(0)
        for j in range(per_owner):
            hit = shard_ref[dst, j] == my_group
            slot = slot_ref[dst, j]
            for k in range(capacity):
                picked[k] = jnp.where(hit & (seen == k), slot, picked[k])
            seen = seen + jnp.where(hit, 1, 0)
        slots.append(picked)

    sources = [shard_ref[my_group, j] for j in range(per_owner)]
    ranks, sides = [], []
    for j in range(per_owner):
        rank = jnp.int32(0)
        for i in range(j):
            rank = rank + jnp.where(sources[i] == sources[j], 1, 0)
        ranks.append(jnp.minimum(rank, capacity - 1))
        sides.append(jnp.where(sources[j] == sources[0], 0, 1))

    fine = rows // 4

    def split_kind(kind):
        row = lax.broadcasted_iota(jnp.int32, (fine, fine * kinds), 0)
        col = lax.broadcasted_iota(jnp.int32, (fine, fine * kinds), 1)
        pick = jnp.where(col == row * kinds + kind, 1.0, 0.0).astype(jnp.bfloat16)

        def one(dst, k, low):
            p = max(p for p, (first, _) in enumerate(pieces) if first <= low)
            at = (low - pieces[p][0]) * kinds
            block = ingest_refs[p][slots[dst][k], at:at + fine * kinds, :]
            return jnp.dot(pick, block, preferred_element_type=jnp.float32).astype(jnp.bfloat16)

        return one

    units = unit_list(capacity, rows)
    half = groups // 2
    low_side = my_group < half
    depth = jnp.where(low_side, half - 1 - my_group, my_group - half)

    def same(e):
        return jnp.where(low_side, half - 1 - e, half + e)

    def other(e):
        return jnp.where(low_side, half + e, half - 1 - e)

    def fill(kind, k, low, size):
        one = split_kind(kind)
        base = (KINDS.index(kind) * capacity + k) * rows
        for dst in range(groups):
            for at in range(low, low + size, fine):
                send_buf[dst, base + at:base + at + fine, :] = one(dst, k, at)

    def span(n):
        kind, _, k, low, size = units[n]
        return pl.ds((KINDS.index(kind) * capacity + k) * rows + low, size)

    def inbox(n, src):
        kind, c, k, low, size = units[n]
        return recv_u[c].at[src] if kind == UPDATE else recv_bufs[FIRST_KINDS.index(kind)].at[src, k, pl.ds(low, size)]

    def keep(kind):
        for n, unit in enumerate(units):
            if unit[0] == kind:
                inbox(n, my_group)[...] = send_buf[my_group, span(n), :]

    def z_copy(src, dst, out_id, in_id, to):
        return pltpu.make_async_remote_copy(
            src_ref=src, dst_ref=dst, send_sem=z_send.at[out_id], recv_sem=z_recv.at[in_id],
            device_id={"batch": to}, device_id_type=MESH)

    def here_id(n):
        kind, c = units[n][:2]
        return 3 + c if kind == UPDATE else FIRST_KINDS.index(kind)

    def relay_id(kind, far, e):
        return 3 + len(chunks) + (KINDS.index(kind) * (half - 1) + far - 1) * half + e

    def side_copy(n, e):
        return z_copy(send_buf.at[same(e), span(n)], inbox(n, my_group), e, here_id(n), same(e))

    def cross_copy(n, e):
        return z_copy(send_buf.at[other(e), span(n)], inbox(n, my_group), half + e, here_id(n), other(e))

    def relay_copy(n, far, e):
        return z_copy(send_buf.at[other(e), span(n)], relay_buf.at[far - 1, e, span(n)],
                      half + e, relay_id(units[n][0], far, e), same(0))

    def forward_copy(n, far, e):
        return z_copy(relay_buf.at[far - 1, e, span(n)], inbox(n, same(far)),
                      2 * half + (far - 1) * half + e, here_id(n), other(e))

    def side(n, middle):
        for here in range(half):
            if (here == 0) == middle and half > 1:
                @pl.when(depth == here)
                def _():
                    for e in range(half):
                        if e != here:
                            side_copy(n, e).start()

    def cross(n, e):
        @pl.when(depth == 0)
        def _():
            cross_copy(n, e).start()

    def to_middle(n, e):
        for here in range(1, half):
            @pl.when(depth == here)
            def _():
                relay_copy(n, here, e).start()

    relayed = set()

    def forward(n, e):
        kind = units[n][0]
        first = (kind, e) not in relayed
        relayed.add((kind, e))
        for far in range(1, half):
            @pl.when(depth == 0)
            def _():
                if first:
                    whole = relay_buf.at[far - 1, e, pl.ds(KINDS.index(kind) * capacity * rows, capacity * rows)]
                    z_copy(whole, whole, 0, relay_id(kind, far, e), my_group).wait_recv()
                forward_copy(n, far, e).start()

    def arrive(buf, in_id):
        others = buf.at[pl.ds(0, groups - 1)]
        z_copy(others, others, 0, in_id, my_group).wait_recv()

    def sent():
        whole = send_buf.at[0]
        for e in range(half):
            @pl.when(depth != e)
            def _():
                z_copy(whole, whole, e, 0, my_group).wait_send()
            z_copy(whole, whole, half + e, 0, my_group).wait_send()
        for flow in range(2 * half, half + half * half):
            @pl.when(depth == 0)
            def _():
                z_copy(whole, whole, flow, 0, my_group).wait_send()

    def collect(kind, own_ref):
        n = FIRST_KINDS.index(kind)
        arrive(recv_bufs[n], n)
        for j in range(per_owner):
            own_ref[j * rows:(j + 1) * rows, :] = recv_bufs[n][sources[j], ranks[j]]

    def hear(distance):
        for there, semaphore in ((my_group >= distance, from_low), (my_group + distance < groups, from_high)):
            @pl.when(there)
            def _():
                pl.semaphore_wait(semaphore.at[distance - 2], 1)

    def pass_on(distance):
        tell((my_group >= distance) & has_high, from_low.at[distance - 1], my_group + 1)
        tell((my_group + distance < groups) & has_low, from_high.at[distance - 1], my_group - 1)

    key_units, value_units, query_units = ([n for n, unit in enumerate(units) if unit[0] == want] for want in FIRST_KINDS)
    update_units = [n for n, unit in enumerate(units) if unit[0] == UPDATE]
    pairs = key_units + value_units
    far_first = list(range(half - 1, -1, -1))
    early = [(n, 0) for n in query_units]
    late_order = [(n, e) for group in (query_units, update_units) for e in far_first for n in group]

    ingest_copies[0].wait()
    fill(KEY, *units[0][2:])
    pl.semaphore_wait(barrier, neighbours + ctxs + heads - 2)
    for n in pairs:
        if n == 1:
            for copy in ingest_copies[1:]:
                copy.wait()
        if n > 0:
            fill(units[n][0], *units[n][2:])
        if n == 1:
            for distance in range(1, half):
                if distance > 1:
                    hear(distance)
                pass_on(distance)
        cross(n, 0)
        if n in key_units:
            to_middle(n, 0)
        side(n, True)
    for e in range(1, half):
        for n in pairs:
            to_middle(n, e)
    for n in value_units:
        to_middle(n, 0)
    for n in pairs:
        side(n, False)
    for n in query_units:
        fill(QUERY, *units[n][2:])
        cross(n, 0)
        side(n, True)
    for k in range(capacity):
        fill(UPDATE, k, 0, rows)
    for n in update_units:
        side(n, True)
    for n, e in late_order:
        to_middle(n, e)
    for n in query_units + update_units:
        side(n, False)
    for kind in KINDS:
        keep(kind)
    if half > 1:
        hear(half)
    for n in key_units:
        forward(n, 0)
    for e in range(1, half):
        for group in (key_units, value_units):
            for n in group:
                cross(n, e)
            for n in group:
                forward(n, e)
    for n in value_units:
        forward(n, 0)

    for copy in local_copies[2:]:
        copy.wait()
    w_copies = []
    for offset in range(1, heads):
        to = lax.rem(my_head + offset, heads)
        copy = pltpu.make_async_remote_copy(
            src_ref=w_ref.at[:, pl.ds(pl.multiple_of(to * HD, HD), HD)], dst_ref=w_cols.at[my_head],
            send_sem=w_send.at[offset - 1], recv_sem=w_recv,
            device_id={"head": to}, device_id_type=MESH)
        copy.start()
        w_copies.append(copy)
    w_cols[my_head] = w_ref[:, pl.ds(pl.multiple_of(my_head * HD, HD), HD)]

    ends, total = [], jnp.int32(0)
    for u in range(hist_ref.shape[0]):
        total = total + hist_ref[u]
        ends.append(total)
    base = my_ctx * row_count
    position = base + lax.broadcasted_iota(jnp.int32, (row_count, HD), 0)
    first = jnp.zeros((row_count, HD), jnp.int32)
    for end in ends:
        first = jnp.where(position >= end, end, first)
    start_ref[...] = first - base

    def ctx_copy(n, own_ref, prev_ref, offset):
        return pltpu.make_async_remote_copy(
            src_ref=own_ref, dst_ref=prev_ref.at[offset - 1],
            send_sem=c_send.at[n, offset - 1], recv_sem=c_recv.at[n, offset - 1],
            device_id={"ctx": lax.rem(my_ctx + offset, ctxs)}, device_id_type=MESH)

    def push(n, own_ref, prev_ref):
        for offset in range(1, window + 1):
            @pl.when(my_ctx + offset < ctxs)
            def _():
                ctx_copy(n, own_ref, prev_ref, offset).start()

    collect(KEY, own_k)
    push(0, own_k, prev_k)
    for n, e in late_order:
        if n in query_units and e > 0:
            cross(n, e)
            forward(n, e)
    collect(VALUE, own_v)
    push(1, own_v, prev_v)
    for n, e in late_order:
        if n in query_units and e > 0:
            continue
        if (n, e) not in early:
            cross(n, e)
        forward(n, e)
    collect(QUERY, own_q)

    tile = 2 * rows if per_owner % 2 == 0 else rows
    tiles = row_count // tile
    half_scale = 0.5 / math.sqrt(HD)

    def attend(q, key_tile, value_tile, q_lo, k_lo, shift, causal):
        scores = lax.dot_general(q, key_tile, (((1,), (1,)), ((), ())), preferred_element_type=jnp.float32)
        half = scores * half_scale
        act = half + half * jnp.tanh(half)
        key_pos = lax.broadcasted_iota(jnp.int32, (tile, tile), 1) + (k_lo - shift)
        first_pos = jnp.concatenate([start_ref[q_lo:q_lo + tile, :]] * (tile // HD), axis=1)
        visible = key_pos >= first_pos
        if causal:
            visible = visible & (key_pos <= lax.broadcasted_iota(jnp.int32, (tile, tile), 0) + q_lo)
        weights = jnp.where(visible, act, 0.0).astype(jnp.bfloat16)
        return jnp.dot(weights, value_tile, preferred_element_type=jnp.float32)

    def put(i, value, add):
        for part in range(tile // rows):
            at = i * (tile // rows) + part
            piece = value[part * rows:(part + 1) * rows]
            att[at] = att[at] + piece if add else piece

    for i in range(tiles):
        q = own_q[i * tile:(i + 1) * tile, :]
        acc = None
        for t in range(i + 1):
            span = slice(t * tile, (t + 1) * tile)
            term = attend(q, own_k[span, :], own_v[span, :], i * tile, t * tile, 0, t == i)
            acc = term if acc is None else acc + term
        put(i, acc, False)
    for offset in range(1, window + 1):
        @pl.when(my_ctx >= offset)
        def _():
            ctx_copy(0, own_k, prev_k, offset).wait_recv()
            ctx_copy(1, own_v, prev_v, offset).wait_recv()
            for i in range(tiles):
                q = own_q[i * tile:(i + 1) * tile, :]
                acc = None
                for t in range(i if offset == window else 0, tiles):
                    span = slice(t * tile, (t + 1) * tile)
                    term = attend(q, prev_k[offset - 1, span, :], prev_v[offset - 1, span, :],
                                  i * tile, t * tile, offset * row_count, False)
                    acc = term if acc is None else acc + term
                put(i, acc, True)

    for j in range(per_owner):
        rows_f32 = att[j]
        mean_square = jnp.mean(rows_f32 * rows_f32, axis=-1, keepdims=True)
        att[j] = rows_f32 * lax.rsqrt(mean_square + 1e-06)

    source_other = sources[0]
    for j in range(1, per_owner):
        source_other = jnp.where(sides[j] == 1, sources[j], source_other)
    side_source = (sources[0], source_other)
    for c, (k, low, size) in enumerate(chunks):
        arrive(recv_u[c], 3 + c)
        for part in range(2):
            at = jnp.int32(0)
            for j in range(per_owner):
                at = jnp.where((ranks[j] == k) & (sides[j] == part), j, at)
            normed = att[at, low:low + size, :]
            update = recv_u[c][side_source[part]].astype(jnp.float32)
            gated[c][my_head, part * size:(part + 1) * size, :] = (normed * update).astype(jnp.bfloat16)
        for offset in range(1, heads):
            copy = pltpu.make_async_remote_copy(
                src_ref=gated[c].at[my_head], dst_ref=gated[c].at[my_head],
                send_sem=h_send.at[offset - 1], recv_sem=h_recv.at[c // TOGETHER],
                device_id={"head": lax.rem(my_head + offset, heads)}, device_id_type=MESH)
            copy.start()
    for copy in w_copies:
        copy.wait_send()
    if heads > 1:
        all_cols = w_cols.at[pl.ds(0, heads - 1)]
        pltpu.make_async_copy(all_cols, all_cols, w_recv).wait()
    sent()
    for c, (k, low, size) in enumerate(chunks):
        if heads > 1 and c % TOGETHER == 0:
            theirs = send_buf.at[0, pl.ds(0, TOGETHER * 2 * size * (heads - 1))]
            pltpu.make_async_copy(theirs, theirs, h_recv.at[c // TOGETHER]).wait()
        acc = None
        for h in range(heads):
            term = jnp.dot(gated[c][h], w_cols[h], preferred_element_type=jnp.float32)
            acc = term if acc is None else acc + term
        acc = acc.astype(jnp.bfloat16)
        for side in range(2):
            mixed[2 * k + side, low:low + size, :] = acc[side * size:(side + 1) * size]
    for offset in range(1, heads):
        pltpu.make_async_remote_copy(
            src_ref=own_q, dst_ref=own_q, send_sem=h_send.at[offset - 1], recv_sem=h_recv.at[0],
            device_id={"head": my_head}, device_id_type=MESH).wait_send()
    for j in range(per_owner):
        out_ref[j * rows:(j + 1) * rows, :] = mixed[2 * ranks[j] + sides[j]]
    for offset in range(1, window + 1):
        @pl.when(my_ctx + offset < ctxs)
        def _():
            ctx_copy(0, own_k, prev_k, offset).wait_send()
            ctx_copy(1, own_v, prev_v, offset).wait_send()


def body(ingest, src_shard, src_slot, hist_len, w_out):
    groups, ctxs, heads = (lax.axis_size(a) for a in ("batch", "ctx", "head"))
    slot_total, rows, kinds, width = ingest.shape[2:]
    per_owner = src_shard.shape[2]
    capacity = per_owner // 2
    chunks = update_chunks(capacity, rows)
    half = groups // 2
    spans = max(half - 1, 1)
    window = ctxs // 2
    row_count = per_owner * rows
    bf16 = jnp.bfloat16
    dma = pltpu.SemaphoreType.DMA
    vmem = pl.BlockSpec(memory_space=pltpu.VMEM)
    mixed = pl.pallas_call(
        functools.partial(kernel, (groups, ctxs, heads, per_owner, rows)),
        out_shape=pltpu.VMEM((row_count, width), bf16),
        in_specs=[pl.BlockSpec(memory_space=pl.ANY)] * 5,
        out_specs=vmem,
        scratch_shapes=[
            pltpu.SMEM(src_shard.shape[1:], jnp.int32), pltpu.SMEM(src_slot.shape[1:], jnp.int32),
            pltpu.SMEM(hist_len.shape[1:], jnp.int32), pltpu.VMEM(w_out.shape, bf16), dma((4,)),
            [pltpu.VMEM((slot_total, size * kinds, width), bf16) for _, size in load_pieces(rows)],
            pltpu.VMEM((groups, 4 * capacity * rows, width), bf16),
            [pltpu.VMEM((groups, capacity, rows, width), bf16)] * 3,
            [pltpu.VMEM((groups, size, width), bf16) for _, _, size in chunks],
            pltpu.VMEM((spans, half, 4 * capacity * rows, width), bf16),
            pltpu.VMEM((row_count, width), bf16),
            pltpu.VMEM((row_count, width), bf16),
            pltpu.VMEM((row_count, width), bf16),
            pltpu.VMEM((window, row_count, width), bf16),
            pltpu.VMEM((window, row_count, width), bf16),
            pltpu.VMEM((row_count, width), jnp.int32),
            pltpu.VMEM((per_owner, rows, width), jnp.float32),
            [pltpu.VMEM((heads, 2 * size, width), bf16) for _, _, size in chunks],
            pltpu.VMEM((heads, width, width), bf16),
            pltpu.VMEM((per_owner, rows, width), bf16),
            dma((groups + spans * half,)), dma((3 + len(chunks) + 4 * spans * half,)),
            dma((2, window)), dma((2, window)),
            dma((max(heads - 1, 1),)), dma((len(chunks) // TOGETHER,)),
            dma((max(heads - 1, 1),)), dma,
            dma((2,)), pltpu.SemaphoreType.REGULAR((spans,)), pltpu.SemaphoreType.REGULAR((spans,)),
        ],
        compiler_params=pltpu.CompilerParams(
            collective_id=0, has_side_effects=True, vmem_limit_bytes=56 * 1024 * 1024),
    )(src_shard[0], src_slot[0], hist_len[0],
      ingest.reshape(slot_total, rows * kinds, width), w_out)
    return mixed[None]


def solution(mesh):
    in_specs = (
        P("ctx", "batch", None, None, None, "head"),
        P("ctx", None, None),
        P("ctx", None, None),
        P("batch", None),
        P("head", None),
    )
    out_specs = P("batch", "ctx", "head")
    return jax.shard_map(body, mesh=mesh, in_specs=in_specs, out_specs=out_specs, check_vma=False)
```

```python
import functools
import math

import jax
import jax.numpy as jnp
from jax import lax
from jax.experimental import pallas as pl
from jax.experimental.pallas import tpu as pltpu
from jax.sharding import PartitionSpec as P

HD = 128
MESH = pl.DeviceIdType.MESH
QUERY, KEY, VALUE, UPDATE = 0, 1, 2, 3
FIRST_KINDS = (KEY, VALUE, QUERY)
KINDS = (*FIRST_KINDS, UPDATE)
SPLIT = 4
TOGETHER = 2


def load_pieces(rows):
    return [(0, rows // 4), (rows // 4, rows - rows // 4)]


def unit_list(capacity, rows):
    units = [(KEY, 0, 0, low, size) for low, size in load_pieces(rows)]
    units += [(KEY, k, k, 0, rows) for k in range(1, capacity)]
    units += [(kind, k, k, 0, rows) for kind in FIRST_KINDS[1:] for k in range(capacity)]
    return units + [(UPDATE, c, *chunk) for c, chunk in enumerate(update_chunks(capacity, rows))]


def update_chunks(capacity, rows):
    size = rows // SPLIT
    return [(k, part * size, size) for k in range(capacity) for part in range(SPLIT)]


def kernel(sizes, shard_hbm, slot_hbm, hist_hbm, ingest_hbm, w_hbm, out_ref,
           shard_ref, slot_ref, hist_ref, w_ref, local_sems,
           ingest_refs,
           send_buf, recv_bufs, recv_u, relay_buf, own_k, own_v, own_q, prev_k, prev_v,
           start_ref, att, gated, w_cols, mixed,
           z_send, z_recv, c_send, c_recv, h_send, h_recv, w_send, w_recv,
           ingest_sems, from_low, from_high):
    groups, ctxs, heads, per_owner, rows = sizes
    capacity = per_owner // 2
    chunks = update_chunks(capacity, rows)
    window = ctxs // 2
    row_count = per_owner * rows
    my_group = lax.axis_index("batch")
    my_ctx = lax.axis_index("ctx")
    my_head = lax.axis_index("head")

    barrier = pltpu.get_barrier_semaphore()
    local_copies = [pltpu.make_async_copy(src, dst, local_sems.at[i]) for i, (src, dst) in enumerate((
        (shard_hbm, shard_ref), (slot_hbm, slot_ref), (hist_hbm, hist_ref), (w_hbm, w_ref)))]
    pieces = load_pieces(rows)
    kinds = ingest_hbm.shape[1] // rows
    ingest_copies = [pltpu.make_async_copy(
        ingest_hbm.at[:, pl.ds(low * kinds, size * kinds), :], ingest_refs[p], ingest_sems.at[p])
        for p, (low, size) in enumerate(pieces)]
    for copy in (*local_copies[:2], *ingest_copies, *local_copies[2:]):
        copy.start()
    for axis, me, count in (("ctx", my_ctx, ctxs), ("head", my_head, heads)):
        for offset in range(1, count):
            pl.semaphore_signal(barrier, inc=1, device_id={axis: lax.rem(me + offset, count)}, device_id_type=MESH)
    has_low, has_high = my_group > 0, my_group < groups - 1

    def tell(there, semaphore, to):
        @pl.when(there)
        def _():
            pl.semaphore_signal(semaphore, inc=1, device_id={"batch": to}, device_id_type=MESH)

    tell(has_low, barrier, my_group - 1)
    tell(has_high, barrier, my_group + 1)
    neighbours = jnp.where(has_low, 1, 0) + jnp.where(has_high, 1, 0)

    for copy in local_copies[:2]:
        copy.wait()
    slots = []
    for dst in range(groups):
        picked = [jnp.int32(0)] * capacity
        seen = jnp.int32(0)
        for j in range(per_owner):
            hit = shard_ref[dst, j] == my_group
            slot = slot_ref[dst, j]
            for k in range(capacity):
                picked[k] = jnp.where(hit & (seen == k), slot, picked[k])
            seen = seen + jnp.where(hit, 1, 0)
        slots.append(picked)

    sources = [shard_ref[my_group, j] for j in range(per_owner)]
    ranks, sides = [], []
    for j in range(per_owner):
        rank = jnp.int32(0)
        for i in range(j):
            rank = rank + jnp.where(sources[i] == sources[j], 1, 0)
        ranks.append(jnp.minimum(rank, capacity - 1))
        sides.append(jnp.where(sources[j] == sources[0], 0, 1))

    fine = rows // 4

    def split_kind(kind):
        row = lax.broadcasted_iota(jnp.int32, (fine, fine * kinds), 0)
        col = lax.broadcasted_iota(jnp.int32, (fine, fine * kinds), 1)
        pick = jnp.where(col == row * kinds + kind, 1.0, 0.0).astype(jnp.bfloat16)

        def one(dst, k, low):
            p = max(p for p, (first, _) in enumerate(pieces) if first <= low)
            at = (low - pieces[p][0]) * kinds
            block = ingest_refs[p][slots[dst][k], at:at + fine * kinds, :]
            return jnp.dot(pick, block, preferred_element_type=jnp.float32).astype(jnp.bfloat16)

        return one

    units = unit_list(capacity, rows)
    half = groups // 2
    low_side = my_group < half
    depth = jnp.where(low_side, half - 1 - my_group, my_group - half)

    def same(e):
        return jnp.where(low_side, half - 1 - e, half + e)

    def other(e):
        return jnp.where(low_side, half + e, half - 1 - e)

    def fill(kind, k, low, size):
        one = split_kind(kind)
        base = (KINDS.index(kind) * capacity + k) * rows
        for dst in range(groups):
            for at in range(low, low + size, fine):
                send_buf[dst, base + at:base + at + fine, :] = one(dst, k, at)

    def span(n):
        kind, _, k, low, size = units[n]
        return pl.ds((KINDS.index(kind) * capacity + k) * rows + low, size)

    def inbox(n, src):
        kind, c, k, low, size = units[n]
        return recv_u[c].at[src] if kind == UPDATE else recv_bufs[FIRST_KINDS.index(kind)].at[src, k, pl.ds(low, size)]

    def keep(kind):
        for n, unit in enumerate(units):
            if unit[0] == kind:
                inbox(n, my_group)[...] = send_buf[my_group, span(n), :]

    def z_copy(src, dst, out_id, in_id, to):
        return pltpu.make_async_remote_copy(
            src_ref=src, dst_ref=dst, send_sem=z_send.at[out_id], recv_sem=z_recv.at[in_id],
            device_id={"batch": to}, device_id_type=MESH)

    def here_id(n):
        kind, c = units[n][:2]
        return 3 + c if kind == UPDATE else FIRST_KINDS.index(kind)

    def relay_id(kind, far, e):
        return 3 + len(chunks) + (KINDS.index(kind) * (half - 1) + far - 1) * half + e

    def side_copy(n, e):
        return z_copy(send_buf.at[same(e), span(n)], inbox(n, my_group), e, here_id(n), same(e))

    def cross_copy(n, e):
        return z_copy(send_buf.at[other(e), span(n)], inbox(n, my_group), half + e, here_id(n), other(e))

    def relay_copy(n, far, e):
        return z_copy(send_buf.at[other(e), span(n)], relay_buf.at[far - 1, e, span(n)],
                      half + e, relay_id(units[n][0], far, e), same(0))

    def forward_copy(n, far, e):
        return z_copy(relay_buf.at[far - 1, e, span(n)], inbox(n, same(far)),
                      2 * half + (far - 1) * half + e, here_id(n), other(e))

    def side(n, middle):
        for here in range(half):
            if (here == 0) == middle and half > 1:
                @pl.when(depth == here)
                def _():
                    for e in range(half):
                        if e != here:
                            side_copy(n, e).start()

    def cross(n, e):
        @pl.when(depth == 0)
        def _():
            cross_copy(n, e).start()

    def to_middle(n, e):
        for here in range(1, half):
            @pl.when(depth == here)
            def _():
                relay_copy(n, here, e).start()

    relayed = set()

    def forward(n, e):
        kind = units[n][0]
        first = (kind, e) not in relayed
        relayed.add((kind, e))
        for far in range(1, half):
            @pl.when(depth == 0)
            def _():
                if first:
                    whole = relay_buf.at[far - 1, e, pl.ds(KINDS.index(kind) * capacity * rows, capacity * rows)]
                    z_copy(whole, whole, 0, relay_id(kind, far, e), my_group).wait_recv()
                forward_copy(n, far, e).start()

    def arrive(buf, in_id):
        others = buf.at[pl.ds(0, groups - 1)]
        z_copy(others, others, 0, in_id, my_group).wait_recv()

    def sent():
        whole = send_buf.at[0]
        for e in range(half):
            @pl.when(depth != e)
            def _():
                z_copy(whole, whole, e, 0, my_group).wait_send()
            z_copy(whole, whole, half + e, 0, my_group).wait_send()
        for flow in range(2 * half, half + half * half):
            @pl.when(depth == 0)
            def _():
                z_copy(whole, whole, flow, 0, my_group).wait_send()

    def collect(kind, own_ref):
        n = FIRST_KINDS.index(kind)
        arrive(recv_bufs[n], n)
        for j in range(per_owner):
            own_ref[j * rows:(j + 1) * rows, :] = recv_bufs[n][sources[j], ranks[j]]

    def hear(distance):
        for there, semaphore in ((my_group >= distance, from_low), (my_group + distance < groups, from_high)):
            @pl.when(there)
            def _():
                pl.semaphore_wait(semaphore.at[distance - 2], 1)

    def pass_on(distance):
        tell((my_group >= distance) & has_high, from_low.at[distance - 1], my_group + 1)
        tell((my_group + distance < groups) & has_low, from_high.at[distance - 1], my_group - 1)

    key_units, value_units, query_units = ([n for n, unit in enumerate(units) if unit[0] == want] for want in FIRST_KINDS)
    update_units = [n for n, unit in enumerate(units) if unit[0] == UPDATE]
    pairs = key_units + value_units
    far_first = list(range(half - 1, -1, -1))
    early = [(n, 0) for n in query_units]
    late_order = [(n, e) for group in (query_units, update_units) for e in far_first for n in group]

    ingest_copies[0].wait()
    fill(KEY, *units[0][2:])
    pl.semaphore_wait(barrier, neighbours + ctxs + heads - 2)
    for n in pairs:
        if n == 1:
            for copy in ingest_copies[1:]:
                copy.wait()
        if n > 0:
            fill(units[n][0], *units[n][2:])
        if n == 1:
            for distance in range(1, half):
                if distance > 1:
                    hear(distance)
                pass_on(distance)
        cross(n, 0)
        if n in key_units:
            to_middle(n, 0)
        side(n, True)
    for e in range(1, half):
        for n in pairs:
            to_middle(n, e)
    for n in value_units:
        to_middle(n, 0)
    for n in pairs:
        side(n, False)
    for n in query_units:
        fill(QUERY, *units[n][2:])
        cross(n, 0)
        side(n, True)
    for k in range(capacity):
        fill(UPDATE, k, 0, rows)
    for n in update_units:
        side(n, True)
    for n, e in late_order:
        to_middle(n, e)
    for n in query_units + update_units:
        side(n, False)
    for kind in KINDS:
        keep(kind)
    if half > 1:
        hear(half)
    for n in key_units:
        forward(n, 0)
    for e in range(1, half):
        for group in (key_units, value_units):
            for n in group:
                cross(n, e)
            for n in group:
                forward(n, e)
    for n in value_units:
        forward(n, 0)

    for copy in local_copies[2:]:
        copy.wait()
    w_copies = []
    for offset in range(1, heads):
        to = lax.rem(my_head + offset, heads)
        copy = pltpu.make_async_remote_copy(
            src_ref=w_ref.at[:, pl.ds(pl.multiple_of(to * HD, HD), HD)], dst_ref=w_cols.at[my_head],
            send_sem=w_send.at[offset - 1], recv_sem=w_recv,
            device_id={"head": to}, device_id_type=MESH)
        copy.start()
        w_copies.append(copy)
    w_cols[my_head] = w_ref[:, pl.ds(pl.multiple_of(my_head * HD, HD), HD)]

    ends, total = [], jnp.int32(0)
    for u in range(hist_ref.shape[0]):
        total = total + hist_ref[u]
        ends.append(total)
    base = my_ctx * row_count
    position = base + lax.broadcasted_iota(jnp.int32, (row_count, HD), 0)
    first = jnp.zeros((row_count, HD), jnp.int32)
    for end in ends:
        first = jnp.where(position >= end, end, first)
    start_ref[...] = first - base

    def ctx_copy(n, own_ref, prev_ref, offset):
        return pltpu.make_async_remote_copy(
            src_ref=own_ref, dst_ref=prev_ref.at[offset - 1],
            send_sem=c_send.at[n, offset - 1], recv_sem=c_recv.at[n, offset - 1],
            device_id={"ctx": lax.rem(my_ctx + offset, ctxs)}, device_id_type=MESH)

    def push(n, own_ref, prev_ref):
        for offset in range(1, window + 1):
            @pl.when(my_ctx + offset < ctxs)
            def _():
                ctx_copy(n, own_ref, prev_ref, offset).start()

    collect(KEY, own_k)
    push(0, own_k, prev_k)
    for n, e in late_order:
        if n in query_units and e > 0:
            cross(n, e)
            forward(n, e)
    collect(VALUE, own_v)
    push(1, own_v, prev_v)
    for n, e in late_order:
        if n in query_units and e > 0:
            continue
        if (n, e) not in early:
            cross(n, e)
        forward(n, e)
    collect(QUERY, own_q)

    tile = 2 * rows if per_owner % 2 == 0 else rows
    tiles = row_count // tile
    half_scale = 0.5 / math.sqrt(HD)

    def attend(q, key_tile, value_tile, q_lo, k_lo, shift, causal):
        scores = lax.dot_general(q, key_tile, (((1,), (1,)), ((), ())), preferred_element_type=jnp.float32)
        half = scores * half_scale
        act = half + half * jnp.tanh(half)
        key_pos = lax.broadcasted_iota(jnp.int32, (tile, tile), 1) + (k_lo - shift)
        first_pos = jnp.concatenate([start_ref[q_lo:q_lo + tile, :]] * (tile // HD), axis=1)
        visible = key_pos >= first_pos
        if causal:
            visible = visible & (key_pos <= lax.broadcasted_iota(jnp.int32, (tile, tile), 0) + q_lo)
        weights = jnp.where(visible, act, 0.0).astype(jnp.bfloat16)
        return jnp.dot(weights, value_tile, preferred_element_type=jnp.float32)

    def put(i, value, add):
        for part in range(tile // rows):
            at = i * (tile // rows) + part
            piece = value[part * rows:(part + 1) * rows]
            att[at] = att[at] + piece if add else piece

    for i in range(tiles):
        q = own_q[i * tile:(i + 1) * tile, :]
        acc = None
        for t in range(i + 1):
            span = slice(t * tile, (t + 1) * tile)
            term = attend(q, own_k[span, :], own_v[span, :], i * tile, t * tile, 0, t == i)
            acc = term if acc is None else acc + term
        put(i, acc, False)
    for offset in range(1, window + 1):
        @pl.when(my_ctx >= offset)
        def _():
            ctx_copy(0, own_k, prev_k, offset).wait_recv()
            ctx_copy(1, own_v, prev_v, offset).wait_recv()
            for i in range(tiles):
                q = own_q[i * tile:(i + 1) * tile, :]
                acc = None
                for t in range(i if offset == window else 0, tiles):
                    span = slice(t * tile, (t + 1) * tile)
                    term = attend(q, prev_k[offset - 1, span, :], prev_v[offset - 1, span, :],
                                  i * tile, t * tile, offset * row_count, False)
                    acc = term if acc is None else acc + term
                put(i, acc, True)

    for j in range(per_owner):
        rows_f32 = att[j]
        mean_square = jnp.mean(rows_f32 * rows_f32, axis=-1, keepdims=True)
        att[j] = rows_f32 * lax.rsqrt(mean_square + 1e-06)

    source_other = sources[0]
    for j in range(1, per_owner):
        source_other = jnp.where(sides[j] == 1, sources[j], source_other)
    side_source = (sources[0], source_other)
    for c, (k, low, size) in enumerate(chunks):
        arrive(recv_u[c], 3 + c)
        for part in range(2):
            at = jnp.int32(0)
            for j in range(per_owner):
                at = jnp.where((ranks[j] == k) & (sides[j] == part), j, at)
            normed = att[at, low:low + size, :]
            update = recv_u[c][side_source[part]].astype(jnp.float32)
            gated[c][my_head, part * size:(part + 1) * size, :] = (normed * update).astype(jnp.bfloat16)
        for offset in range(1, heads):
            copy = pltpu.make_async_remote_copy(
                src_ref=gated[c].at[my_head], dst_ref=gated[c].at[my_head],
                send_sem=h_send.at[offset - 1], recv_sem=h_recv.at[c // TOGETHER],
                device_id={"head": lax.rem(my_head + offset, heads)}, device_id_type=MESH)
            copy.start()
    for copy in w_copies:
        copy.wait_send()
    if heads > 1:
        all_cols = w_cols.at[pl.ds(0, heads - 1)]
        pltpu.make_async_copy(all_cols, all_cols, w_recv).wait()
    sent()
    for offset in range(1, window + 1):
        @pl.when(my_ctx + offset < ctxs)
        def _():
            ctx_copy(0, own_k, prev_k, offset).wait_send()
            ctx_copy(1, own_v, prev_v, offset).wait_send()
    for c, (k, low, size) in enumerate(chunks):
        if heads > 1 and c % TOGETHER == 0:
            theirs = send_buf.at[0, pl.ds(0, TOGETHER * 2 * size * (heads - 1))]
            pltpu.make_async_copy(theirs, theirs, h_recv.at[c // TOGETHER]).wait()
        acc = None
        for h in range(heads):
            term = jnp.dot(gated[c][h], w_cols[h], preferred_element_type=jnp.float32)
            acc = term if acc is None else acc + term
        acc = acc.astype(jnp.bfloat16)
        for side in range(2):
            mixed[2 * k + side, low:low + size, :] = acc[side * size:(side + 1) * size]
    for offset in range(1, heads):
        pltpu.make_async_remote_copy(
            src_ref=own_q, dst_ref=own_q, send_sem=h_send.at[offset - 1], recv_sem=h_recv.at[0],
            device_id={"head": my_head}, device_id_type=MESH).wait_send()
    for j in range(per_owner):
        out_ref[j * rows:(j + 1) * rows, :] = mixed[2 * ranks[j] + sides[j]]


def body(ingest, src_shard, src_slot, hist_len, w_out):
    groups, ctxs, heads = (lax.axis_size(a) for a in ("batch", "ctx", "head"))
    slot_total, rows, kinds, width = ingest.shape[2:]
    per_owner = src_shard.shape[2]
    capacity = per_owner // 2
    chunks = update_chunks(capacity, rows)
    half = groups // 2
    spans = max(half - 1, 1)
    window = ctxs // 2
    row_count = per_owner * rows
    bf16 = jnp.bfloat16
    dma = pltpu.SemaphoreType.DMA
    vmem = pl.BlockSpec(memory_space=pltpu.VMEM)
    mixed = pl.pallas_call(
        functools.partial(kernel, (groups, ctxs, heads, per_owner, rows)),
        out_shape=pltpu.VMEM((row_count, width), bf16),
        in_specs=[pl.BlockSpec(memory_space=pl.ANY)] * 5,
        out_specs=vmem,
        scratch_shapes=[
            pltpu.SMEM(src_shard.shape[1:], jnp.int32), pltpu.SMEM(src_slot.shape[1:], jnp.int32),
            pltpu.SMEM(hist_len.shape[1:], jnp.int32), pltpu.VMEM(w_out.shape, bf16), dma((4,)),
            [pltpu.VMEM((slot_total, size * kinds, width), bf16) for _, size in load_pieces(rows)],
            pltpu.VMEM((groups, 4 * capacity * rows, width), bf16),
            [pltpu.VMEM((groups, capacity, rows, width), bf16)] * 3,
            [pltpu.VMEM((groups, size, width), bf16) for _, _, size in chunks],
            pltpu.VMEM((spans, half, 4 * capacity * rows, width), bf16),
            pltpu.VMEM((row_count, width), bf16),
            pltpu.VMEM((row_count, width), bf16),
            pltpu.VMEM((row_count, width), bf16),
            pltpu.VMEM((window, row_count, width), bf16),
            pltpu.VMEM((window, row_count, width), bf16),
            pltpu.VMEM((row_count, width), jnp.int32),
            pltpu.VMEM((per_owner, rows, width), jnp.float32),
            [pltpu.VMEM((heads, 2 * size, width), bf16) for _, _, size in chunks],
            pltpu.VMEM((heads, width, width), bf16),
            pltpu.VMEM((per_owner, rows, width), bf16),
            dma((groups + spans * half,)), dma((3 + len(chunks) + 4 * spans * half,)),
            dma((2, window)), dma((2, window)),
            dma((max(heads - 1, 1),)), dma((len(chunks) // TOGETHER,)),
            dma((max(heads - 1, 1),)), dma,
            dma((2,)), pltpu.SemaphoreType.REGULAR((spans,)), pltpu.SemaphoreType.REGULAR((spans,)),
        ],
        compiler_params=pltpu.CompilerParams(
            collective_id=0, has_side_effects=True, vmem_limit_bytes=56 * 1024 * 1024),
    )(src_shard[0], src_slot[0], hist_len[0],
      ingest.reshape(slot_total, rows * kinds, width), w_out)
    return mixed[None]


def solution(mesh):
    in_specs = (
        P("ctx", "batch", None, None, None, "head"),
        P("ctx", None, None),
        P("ctx", None, None),
        P("batch", None),
        P("head", None),
    )
    out_specs = P("batch", "ctx", "head")
    return jax.shard_map(body, mesh=mesh, in_specs=in_specs, out_specs=out_specs, check_vma=False)
```
